256 devices in a mesh: shard: 64 (over z, x_lo, y), blk: 4 (over x_hi, core).
Axes of the slice: x: 4 (x_hi: 2, x_lo: 2; x = x_hi * 2 + x_lo), y: 4, z: 8, core: 2. Of those that a mesh axis runs over, the one named last changes fastest.
Arguments:
- embeddings: bfloat16 [65536, 1024], P(('shard', 'blk')), may hold values from -6 to 6
- doc_cluster: int32 [65536], P(('shard', 'blk')), may hold values from 0 to 255, as said below
- doc_valid: int32 [65536], P(('shard', 'blk')), may hold values 0 or 1
Outputs:
- max_similar: float32 [65536], P(('shard', 'blk'))
The draws below stay inside these ranges and needn't reach their ends.
Inputs may be any that keep to these rules, and one draw needn't show every extreme that they name: `doc_cluster`: among the documents of one device at most 16 have clusters of one owner group (cluster mod 64), and at most 4 have clusters c of one owner group with one value of (c // 64) mod 4; one owner group, the same on every device, gets exactly 16 from every device, 4 for each such value.
All inputs are finite; a program needn't handle non-finite values. No bound on the sum of `doc_valid` on one device may be relied on, other than what follows from the above.
Results may differ from the reference program's by a relative error of at most 0.00036.
Values may be sent and summed in bfloat16 or wider, within the bound.
A program may use at most 64 MiB of HBM per device.

```python
import math
import jax
import jax.numpy as jnp
from jax import lax

E = 1024
DOC_DEV = 256
CL_OWN = 4
CAP = 16
DOCS = 65536
N_SHARD = 64
N_BLK = 4


def draw_doc_cluster(key, part):
    busy_key, device_key = jax.random.split(jax.random.fold_in(key, 11))
    busiest = jax.random.randint(busy_key, (), 0, N_SHARD).astype(jnp.int32)
    sub_size = CAP // N_BLK

    def per_device(device_seed):
        spread_key, order_key, pick_key = jax.random.split(device_seed, 3)
        picked = jax.random.permutation(spread_key, (N_SHARD - 1) * CAP)[:DOC_DEV - CAP].astype(jnp.int32)
        others = (picked // CAP).astype(jnp.int32)
        others = others + (others >= busiest).astype(jnp.int32)
        other_subs = (picked % CAP // sub_size).astype(jnp.int32)
        owners = jnp.concatenate([jnp.full((CAP,), busiest, jnp.int32), others])
        subs = jnp.concatenate([(jnp.arange(CAP, dtype=jnp.int32) // sub_size).astype(jnp.int32), other_subs])
        extra = jax.random.randint(pick_key, (DOC_DEV,), 0, CL_OWN // N_BLK).astype(jnp.int32)
        clusters = owners + N_SHARD * (subs + N_BLK * extra)
        return clusters[jax.random.permutation(order_key, DOC_DEV)]
    device_keys = jax.random.split(device_key, N_SHARD * N_BLK)
    return jax.vmap(per_device)(device_keys).reshape(DOC_DEV * N_SHARD * N_BLK).astype(jnp.int32)


def touch_ends(drawn, own_key, low, high):
    dims = drawn.shape
    place = [jax.random.randint(jax.random.fold_in(own_key, axis), (), 0, dims[axis]) for axis in range(len(dims))]
    drawn = drawn.at[tuple(place)].set(low)
    longest = dims.index(max(dims))
    place[longest] = (place[longest] + 1) % dims[longest]
    return drawn.at[tuple(place)].set(high)


def block_scale(stream_key, shape, cuts, low, top_value):
    factor_of, own = 1.0, jax.random.fold_in(stream_key, 6)
    for dim, parts in cuts:
        steps = jnp.exp(jax.random.uniform(jax.random.fold_in(own, dim), (parts,), jnp.float32, low / len(cuts), top_value / len(cuts)))
        factor_of = factor_of * jnp.repeat(steps, shape[dim] // parts).reshape([-1 if axis == dim else 1 for axis in range(len(shape))])
    return factor_of


def centred(stream_key, extent, deviation, reach, shards=(), held_as=jnp.bfloat16):
    gain = block_scale(stream_key, extent, shards, -0.22, 0.18) if shards else 1.0
    values = jax.random.normal(stream_key, extent, jnp.float32) * deviation * gain
    return jnp.minimum(jnp.maximum(values, -reach), reach).astype(held_as)


def setup_inputs(seed: int = 0) -> dict:
    splits = jax.random.split(jax.random.key(seed), 4)
    return {
        "embeddings": centred(splits[0], (DOCS, E), 1.0, 6.0, ((0, 256),)),
        "doc_cluster": draw_doc_cluster(jax.random.fold_in(splits[3], 71), 0),
        "doc_valid": touch_ends((jax.random.randint(splits[2], (DOCS,), 0, 8) < 7).astype(jnp.int32), jax.random.fold_in(splits[2], 1), 0, 1),
    }


def unit_rows(embeddings):
    values = embeddings.astype(jnp.float32)
    scale = lax.rsqrt(lax.optimization_barrier(jnp.mean(values * values, axis=1, keepdims=True)) + 1e-05) / math.sqrt(values.shape[1])
    return (values * scale).astype(jnp.bfloat16)

def block_best(rows, keys, idents):
    count_rows = rows.shape[0]
    block_rows = 512 if count_rows % 512 == 0 else count_rows
    rows_wide = rows.astype(jnp.float32)

    def one_block(block):
        rows_query, keys_query, ids_query = block
        similar = jnp.dot(rows_query, rows_wide.T, preferred_element_type=jnp.float32)
        same_group = (keys_query[:, None] == keys[None, :]) & (keys_query[:, None] >= 0) & (ids_query[:, None] != idents[None, :])
        return lax.optimization_barrier(jnp.max(jnp.where(same_group, similar, -1.0), axis=1))
    stacked = (rows_wide.reshape(count_rows // block_rows, block_rows, -1), keys.reshape(count_rows // block_rows, block_rows), idents.reshape(count_rows // block_rows, block_rows))
    return lax.map(one_block, stacked).reshape(count_rows)

def reference(embeddings, doc_cluster, doc_valid):
    doc_count = embeddings.shape[0]
    window = N_BLK * N_SHARD * CAP
    unit = unit_rows(embeddings)
    keyed = jnp.where(doc_valid > 0, doc_cluster, -1).astype(jnp.int32)
    owner = (doc_cluster % N_SHARD).astype(jnp.int32)
    order = jnp.argsort(owner, stable=True).astype(jnp.int32)
    owner_sorted = jnp.concatenate([owner[order], jnp.full((window,), -1, jnp.int32)])
    rows_sorted = jnp.concatenate([unit[order], jnp.zeros((window, unit.shape[1]), jnp.bfloat16)])
    keys_sorted = jnp.concatenate([keyed[order], jnp.full((window,), -1, jnp.int32)])
    ids_sorted = jnp.concatenate([order, jnp.full((window,), doc_count, jnp.int32)])
    counts = lax.optimization_barrier(jnp.sum((owner[None, :] == jnp.arange(N_SHARD, dtype=jnp.int32)[:, None]).astype(jnp.int32), axis=1))
    starts = (jnp.cumsum(counts) - counts).astype(jnp.int32)

    def per_owner(owner_index):
        first_row = starts[owner_index]
        rows_here = lax.dynamic_slice_in_dim(rows_sorted, first_row, window, 0)
        owners_here = lax.dynamic_slice_in_dim(owner_sorted, first_row, window, 0)
        keys_here = lax.dynamic_slice_in_dim(keys_sorted, first_row, window, 0)
        ids_here = lax.dynamic_slice_in_dim(ids_sorted, first_row, window, 0)
        member = owners_here == owner_index
        keys_here = jnp.where(member, keys_here, -1)
        best = block_best(rows_here, keys_here, ids_here)
        target = jnp.where(member, ids_here, doc_count).astype(jnp.int32)
        return (best, target)
    values, targets = lax.map(per_owner, jnp.arange(N_SHARD, dtype=jnp.int32))
    result = jnp.full((doc_count + 1,), -1.0, jnp.float32).at[targets.reshape(-1)].max(values.reshape(-1))
    return result[:doc_count]
```

```python
import functools
import math

import jax
import jax.numpy as jnp
from jax import lax
from jax.experimental import pallas as pl
from jax.experimental.pallas import tpu as pltpu
from jax.sharding import PartitionSpec as P

MESH = pl.DeviceIdType.MESH
PLANES = 8
PEERS = 32
GROUPS = 4
EMPTY = 2.0
FAR = -8.0

PAIRS = ((0, 1), (7, 2), (6, 3), (5, 4))
ORDER = (1, 7, 0, 2, 6, 3, 5, 4)


def iota(shape, dim):
    return lax.broadcasted_iota(jnp.int32, shape, dim)


def as_f32(mask):
    return mask.astype(jnp.float32)


def kernel(
    cap,
    emb_ref,
    clus_ref,
    valid_ref,
    out_ref,
    flag_ref,
    zsend,
    zmeta_send,
    zbuf,
    zmeta,
    psend,
    pbuf,
    bias,
    best,
    ret_send,
    ret_buf,
    zret_send,
    zret_buf,
    zs_sem,
    zr_sem,
    zms_sem,
    zmr_sem,
    ps_sem,
    pr_sem,
    loc_sem,
    rs_sem,
    rr_sem,
    zrs_sem,
    zrr_sem,
):
    docs, width = emb_ref.shape
    shard, blk = lax.axis_index("shard"), lax.axis_index("blk")
    my_z = shard // PLANES
    my_p = lax.rem(shard, PLANES) * 4 + blk

    def at(z, p):
        return (z * PLANES + p // 4, lax.rem(p, 4))

    def z_peer(d):
        return at(lax.rem(my_z + d, PLANES), my_p)

    def p_peer(p):
        return at(my_z, p)

    barrier = pltpu.get_barrier_semaphore()
    for d in range(1, PLANES):
        pl.semaphore_signal(barrier, inc=1, device_id=z_peer(d), device_id_type=MESH)

    def greet(i, carry):
        peer = lax.rem(my_p + i, PEERS)
        pl.semaphore_signal(barrier, inc=1, device_id=p_peer(peer), device_id_type=MESH)
        return carry

    lax.fori_loop(1, PEERS, greet, 0)

    clus = clus_ref[...]
    valid = valid_ref[...] > 0
    owner, sub = clus & 63, clus >> 6
    plane = ((owner >> 3) + 2 * sub) & (PLANES - 1)
    peer_of = (owner & 7) * 4 + sub
    rel = (plane - my_z + PLANES) & (PLANES - 1)
    rel_row = as_f32(jnp.where(valid, rel, -1))
    key_row = as_f32(jnp.where(valid, clus, -1))
    sub_i, lane_i = iota((docs, docs), 0), iota((docs, docs), 1)
    eye = sub_i == lane_i
    earlier = sub_i < lane_i

    def column(row):
        wide = jnp.broadcast_to(row, (docs, docs))
        return jnp.sum(jnp.where(eye, wide, 0.0), axis=1, keepdims=True)

    key_col, rel_col = column(key_row), column(rel_row)
    rank = jnp.sum(as_f32((key_col == key_row) & earlier), axis=0, keepdims=True)
    rank_z = jnp.sum(as_f32((rel_col == rel_row) & earlier), axis=0, keepdims=True)
    slot = as_f32(peer_of * 8) + rank
    slot_bf = jnp.broadcast_to(
        jnp.where(valid, slot + 1.0, 0.0), (8, docs)
    ).astype(jnp.bfloat16)
    fits = valid & (rank_z < float(cap))
    overflow = jnp.max(as_f32(valid & (rank_z >= float(cap))), axis=1, keepdims=True)
    target = jnp.where(fits, rel_row * float(cap) + rank_z, -1.0)

    values = emb_ref[...].astype(jnp.float32)
    scale = lax.rsqrt(jnp.mean(values * values, axis=1, keepdims=True) + 1e-05) / math.sqrt(width)
    unit = (values * scale).astype(jnp.bfloat16)

    pl.semaphore_wait(barrier, PLANES - 1 + PEERS - 1)

    def z_copies(d):
        g, h = place(d)
        rows = pltpu.make_async_remote_copy(
            src_ref=zsend.at[d],
            dst_ref=zbuf.at[g, h],
            send_sem=zs_sem.at[d],
            recv_sem=zr_sem.at[d],
            device_id=z_peer(d),
            device_id_type=MESH,
        )
        meta = pltpu.make_async_remote_copy(
            src_ref=zmeta_send.at[d],
            dst_ref=zmeta.at[d],
            send_sem=zms_sem.at[d],
            recv_sem=zmr_sem.at[d],
            device_id=z_peer(d),
            device_id_type=MESH,
        )
        return rows, meta

    lane128 = iota((1, 128), 1)
    for d in ORDER:
        g, h = place(d)
        pick = iota((cap, docs), 0).astype(jnp.float32) + float(d * cap) == target
        pick = as_f32(pick).astype(jnp.bfloat16)
        rows = jnp.dot(pick, unit, preferred_element_type=jnp.float32).astype(jnp.bfloat16)
        meta = lax.dot_general(
            slot_bf, pick, (((1,), (1,)), ((), ())), preferred_element_type=jnp.float32
        )[0:1, :]
        if d == 0:
            zbuf[g, h] = rows
            zmeta[d, :, 0:cap] = meta
            zmeta[d, :, 128:256] = jnp.broadcast_to(overflow, (1, 128))
        else:
            zsend[d] = rows
            zmeta_send[d, :, 0:cap] = meta
            zmeta_send[d, :, 128:256] = jnp.broadcast_to(overflow, (1, 128))
            row_copy, meta_copy = z_copies(d)
            meta_copy.start()
            row_copy.start()

    best[...] = jnp.full(best.shape, -1.0, jnp.float32)
    slot_lane = iota((PEERS * 8, cap), 0).astype(jnp.float32)
    flag = jnp.zeros((1, 128), jnp.float32)

    def scatter(g):
        picks = []
        flags = []
        for h, d in enumerate(PAIRS[g]):
            if d:
                row_copy, meta_copy = z_copies(d)
                meta_copy.wait_recv()
                row_copy.wait_recv()
            meta = zmeta[d, :, 0:cap]
            where_to = jnp.where(meta > 0.0, meta - 1.0 + float(4 * h), -1.0)
            picks.append(as_f32(slot_lane == where_to))
            flags.append(zmeta[d, :, 128:256])
        pick = jnp.concatenate(picks, axis=1)
        filled = jnp.sum(pick, axis=1, keepdims=True)
        rows = jnp.dot(
            pick.astype(jnp.bfloat16),
            zbuf[g].reshape(2 * cap, width),
            preferred_element_type=jnp.float32,
        )
        mark = jnp.where(iota((PEERS * 8, 128), 1) == 0, EMPTY * (1.0 - filled), 0.0)
        psend[g, :, :, 0:128] = (rows[:, 0:128] + mark).astype(jnp.bfloat16).reshape(PEERS, 8, 128)
        psend[g, :, :, 128:] = rows[:, 128:].astype(jnp.bfloat16).reshape(PEERS, 8, width - 128)
        local = pltpu.make_async_copy(psend.at[g, my_p], pbuf.at[g, my_p], loc_sem.at[g])
        local.start()

        def send(i, carry):
            peer = lax.rem(my_p + i, PEERS)
            pltpu.make_async_remote_copy(
                src_ref=psend.at[g, peer],
                dst_ref=pbuf.at[g, my_p],
                send_sem=ps_sem.at[g],
                recv_sem=pr_sem.at[g],
                device_id=p_peer(peer),
                device_id_type=MESH,
            ).start()
            return carry

        lax.fori_loop(1, PEERS, send, 0)
        return jnp.maximum(flags[0], flags[1])

    def all_in_plane(src, dst, send_sem, recv_sem):
        return pltpu.make_async_remote_copy(
            src_ref=src,
            dst_ref=dst,
            send_sem=send_sem,
            recv_sem=recv_sem,
            device_id=p_peer(lax.rem(my_p + 1, PEERS)),
            device_id_type=MESH,
        )

    def compare(g):
        pltpu.make_async_copy(psend.at[g, my_p], pbuf.at[g, my_p], loc_sem.at[g]).wait()
        all_in_plane(
            psend.at[g, pl.ds(0, PEERS - 1)],
            pbuf.at[g, pl.ds(0, PEERS - 1)],
            ps_sem.at[g],
            pr_sem.at[g],
        ).wait_recv()
        mine = pbuf[g].reshape(PEERS * 8, width)
        first = mine[:, 0:128].astype(jnp.float32)[:, 0:1]
        bias[g] = jnp.broadcast_to(jnp.where(first > 1.5, FAR, 0.0), (PEERS * 8, 128))

        def block(rows_j, rows_i, bias_j, i, same):
            similar = lax.dot_general(
                rows_j, rows_i, (((1,), (1,)), ((), ())), preferred_element_type=jnp.float32
            )
            similar = similar + jnp.concatenate([bias_j, bias_j], axis=1)
            if same:
                similar = jnp.where(eye, FAR, similar)
            best[i] = jnp.maximum(best[i], jnp.max(similar, axis=0, keepdims=True))

        block(mine, mine, bias[g], g, True)
        for j in range(g):
            other = pbuf[j].reshape(PEERS * 8, width)
            block(other, mine, bias[j], g, False)
            block(mine, other, bias[g], j, False)

    for g in range(GROUPS):
        flag = jnp.maximum(flag, scatter(g))
        if g:
            compare(g - 1)
    compare(GROUPS - 1)

    ret_send[...] = jnp.zeros(ret_send.shape, jnp.float32)
    for half in range(2):
        for g in range(GROUPS):
            ret_send[half, g : g + 1, :] = best[g, :, half * 128 : half * 128 + 128]
        ret_send[half, 4:5, :] = flag
    local = pltpu.make_async_copy(ret_send.at[my_p // 16], ret_buf.at[my_p], loc_sem.at[GROUPS])
    local.start()

    def send_back(i, carry):
        peer = lax.rem(my_p + i, PEERS)
        pltpu.make_async_remote_copy(
            src_ref=ret_send.at[peer // 16],
            dst_ref=ret_buf.at[my_p],
            send_sem=rs_sem,
            recv_sem=rr_sem,
            device_id=p_peer(peer),
            device_id_type=MESH,
        ).start()
        return carry

    lax.fori_loop(1, PEERS, send_back, 0)
    local.wait()
    all_in_plane(
        ret_buf.at[pl.ds(0, PEERS - 1)], ret_buf.at[pl.ds(0, PEERS - 1)], rs_sem, rr_sem
    ).wait()
    came = ret_buf[...]
    flag_ref[...] = jnp.max(came[:, 4, :], axis=0, keepdims=True)
    mine = iota((8, 128), 1) == 8 * lax.rem(my_p, 16) + iota((8, 128), 0)
    back = lax.dot_general(
        as_f32(mine),
        came.reshape(PEERS * 8, 128),
        (((1,), (1,)), ((), ())),
        precision=lax.Precision.HIGHEST,
        preferred_element_type=jnp.float32,
    )
    zret_buf[0] = back
    zret_send[...] = back

    def z_back(d):
        return pltpu.make_async_remote_copy(
            src_ref=zret_send,
            dst_ref=zret_buf.at[d],
            send_sem=zrs_sem.at[d],
            recv_sem=zrr_sem.at[d],
            device_id=z_peer(PLANES - d),
            device_id_type=MESH,
        )

    for d in range(1, PLANES):
        z_back(d).start()

    upper = (rel >= 1) & (rel <= 4)
    group = jnp.where(upper, rel - 1, (PLANES - rel) & 7)
    lane_of = as_f32(peer_of * 8 + group)
    row_of = as_f32(rel * 8 + jnp.where(upper, 4, 0)) + rank
    look = as_f32(sub_i.astype(jnp.float32) == lane_of)
    for d in range(1, PLANES):
        z_back(d).wait_recv()
    found = jnp.dot(
        zret_buf[...].reshape(PLANES * 8, PEERS * 8),
        look,
        precision=lax.Precision.HIGHEST,
        preferred_element_type=jnp.float32,
    )
    right = iota((PLANES * 8, docs), 0).astype(jnp.float32) == row_of
    found = jnp.sum(jnp.where(right, found, 0.0), axis=0, keepdims=True)
    out_ref[...] = jnp.where(valid, jnp.maximum(found, -1.0), -1.0)

    for d in range(1, PLANES):
        row_copy, meta_copy = z_copies(d)
        row_copy.wait_send()
        meta_copy.wait_send()
        z_back(d).wait_send()
    for g in range(GROUPS):
        all_in_plane(
            psend.at[g, pl.ds(0, PEERS - 1)],
            pbuf.at[g, pl.ds(0, PEERS - 1)],
            ps_sem.at[g],
            pr_sem.at[g],
        ).wait_send()


def place(d):
    for g, pair in enumerate(PAIRS):
        if d in pair:
            return g, pair.index(d)


def route(cap, collective_id, embeddings, cluster, valid):
    docs, width = embeddings.shape
    vmem = pl.BlockSpec(memory_space=pltpu.VMEM)
    dma = pltpu.SemaphoreType.DMA
    return pl.pallas_call(
        functools.partial(kernel, cap),
        out_shape=(
            jax.ShapeDtypeStruct((1, docs), jnp.float32),
            jax.ShapeDtypeStruct((1, 128), jnp.float32),
        ),
        in_specs=[vmem] * 3,
        out_specs=(vmem, vmem),
        scratch_shapes=[
            pltpu.VMEM((PLANES, cap, width), jnp.bfloat16),
            pltpu.VMEM((PLANES, 1, 256), jnp.float32),
            pltpu.VMEM((GROUPS, 2, cap, width), jnp.bfloat16),
            pltpu.VMEM((PLANES, 1, 256), jnp.float32),
            pltpu.VMEM((GROUPS, PEERS, 8, width), jnp.bfloat16),
            pltpu.VMEM((GROUPS, PEERS, 8, width), jnp.bfloat16),
            pltpu.VMEM((GROUPS, PEERS * 8, 128), jnp.float32),
            pltpu.VMEM((GROUPS, 1, PEERS * 8), jnp.float32),
            pltpu.VMEM((2, 8, 128), jnp.float32),
            pltpu.VMEM((PEERS, 8, 128), jnp.float32),
            pltpu.VMEM((8, PEERS * 8), jnp.float32),
            pltpu.VMEM((PLANES, 8, PEERS * 8), jnp.float32),
            dma((PLANES,)),
            dma((PLANES,)),
            dma((PLANES,)),
            dma((PLANES,)),
            dma((GROUPS,)),
            dma((GROUPS,)),
            dma((GROUPS + 1,)),
            dma(()),
            dma(()),
            dma((PLANES,)),
            dma((PLANES,)),
        ],
        compiler_params=pltpu.CompilerParams(
            collective_id=collective_id, has_side_effects=True, vmem_limit_bytes=40 << 20
        ),
        name=f"route_{cap}",
    )(embeddings, cluster, valid)


def per_device(embeddings, doc_cluster, doc_valid):
    docs = embeddings.shape[0]
    best, _ = route(128, 0, embeddings, doc_cluster.reshape(1, docs), doc_valid.reshape(1, docs))
    return best.reshape(docs)


def solution(mesh):
    placed = (P(("shard", "blk"), None), P(("shard", "blk")), P(("shard", "blk")))
    return jax.shard_map(
        per_device, mesh=mesh, in_specs=placed, out_specs=P(("shard", "blk")), check_vma=False
    )
```

```python
import functools
import math

import jax
import jax.numpy as jnp
from jax import lax
from jax.experimental import pallas as pl
from jax.experimental.pallas import tpu as pltpu
from jax.sharding import PartitionSpec as P

MESH = pl.DeviceIdType.MESH
PLANES = 8
PEERS = 32
GROUPS = 4
EMPTY = 2.0
FAR = -8.0

CAP = 56
MOST = 128

PAIRS = ((0, 1), (7, 2), (6, 3), (5, 4))
ORDER = (1, 7, 0, 2, 6, 3, 5, 4)


def iota(shape, dim):
    return lax.broadcasted_iota(jnp.int32, shape, dim)


def as_f32(mask):
    return mask.astype(jnp.float32)


def kernel(
    cap,
    emb_hbm,
    clus_hbm,
    valid_hbm,
    out_ref,
    flag_ref,
    emb_ref,
    clus_ref,
    valid_ref,
    zsend,
    zmeta_send,
    zbuf,
    zmeta,
    psend,
    pbuf,
    bias,
    best,
    ret_send,
    ret_buf,
    zret_send,
    zret_buf,
    zs_sem,
    zr_sem,
    zms_sem,
    zmr_sem,
    ps_sem,
    pr_sem,
    loc_sem,
    rs_sem,
    rr_sem,
    zrs_sem,
    zrr_sem,
    in_sem,
):
    docs, width = emb_ref.shape
    shard, blk = lax.axis_index("shard"), lax.axis_index("blk")
    my_z = shard // PLANES
    my_p = lax.rem(shard, PLANES) * 4 + blk

    def at(z, p):
        return (z * PLANES + p // 4, lax.rem(p, 4))

    def z_peer(d):
        return at(lax.rem(my_z + d, PLANES), my_p)

    def p_peer(p):
        return at(my_z, p)

    loads = [
        pltpu.make_async_copy(src, dst, in_sem.at[i])
        for i, (src, dst) in enumerate(
            ((emb_hbm, emb_ref), (clus_hbm, clus_ref), (valid_hbm, valid_ref))
        )
    ]
    for load in loads:
        load.start()

    barrier = pltpu.get_barrier_semaphore()
    for d in range(1, PLANES):
        pl.semaphore_signal(barrier, inc=1, device_id=z_peer(d), device_id_type=MESH)

    def greet(i, carry):
        peer = lax.rem(my_p + i, PEERS)
        pl.semaphore_signal(barrier, inc=1, device_id=p_peer(peer), device_id_type=MESH)
        return carry

    lax.fori_loop(1, PEERS, greet, 0)

    for load in loads:
        load.wait()
    clus = clus_ref[...]
    valid = valid_ref[...] > 0
    owner, sub = clus & 63, clus >> 6
    plane = ((owner >> 3) + 2 * sub) & (PLANES - 1)
    peer_of = (owner & 7) * 4 + sub
    rel = (plane - my_z + PLANES) & (PLANES - 1)
    rel_row = as_f32(jnp.where(valid, rel, -1))
    key_row = as_f32(jnp.where(valid, clus, -1))
    sub_i, lane_i = iota((docs, docs), 0), iota((docs, docs), 1)
    eye = sub_i == lane_i
    earlier = sub_i < lane_i

    def column(row):
        wide = jnp.broadcast_to(row, (docs, docs))
        return jnp.sum(jnp.where(eye, wide, 0.0), axis=1, keepdims=True)

    key_col, rel_col = column(key_row), column(rel_row)
    rank = jnp.sum(as_f32((key_col == key_row) & earlier), axis=0, keepdims=True)
    rank_z = jnp.sum(as_f32((rel_col == rel_row) & earlier), axis=0, keepdims=True)
    slot = as_f32(peer_of * 8) + rank
    slot_bf = jnp.broadcast_to(
        jnp.where(valid, slot + 1.0, 0.0), (8, docs)
    ).astype(jnp.bfloat16)
    fits = valid & (rank_z < float(cap))
    overflow = jnp.max(as_f32(valid & (rank_z >= float(cap))), axis=1, keepdims=True)
    target = jnp.where(fits, rel_row * float(cap) + rank_z, -1.0)

    values = emb_ref[...].astype(jnp.float32)
    scale = lax.rsqrt(jnp.mean(values * values, axis=1, keepdims=True) + 1e-05) / math.sqrt(width)
    unit = (values * scale).astype(jnp.bfloat16)

    pl.semaphore_wait(barrier, PLANES - 1 + PEERS - 1)

    def z_copies(d):
        g, h = place(d)
        rows = pltpu.make_async_remote_copy(
            src_ref=zsend.at[d],
            dst_ref=zbuf.at[g, h],
            send_sem=zs_sem.at[d],
            recv_sem=zr_sem.at[d],
            device_id=z_peer(d),
            device_id_type=MESH,
        )
        meta = pltpu.make_async_remote_copy(
            src_ref=zmeta_send.at[d],
            dst_ref=zmeta.at[d],
            send_sem=zms_sem.at[d],
            recv_sem=zmr_sem.at[d],
            device_id=z_peer(d),
            device_id_type=MESH,
        )
        return rows, meta

    lane128 = iota((1, 128), 1)
    for d in ORDER:
        g, h = place(d)
        pick = iota((cap, docs), 0).astype(jnp.float32) + float(d * cap) == target
        pick = as_f32(pick).astype(jnp.bfloat16)
        rows = jnp.dot(pick, unit, preferred_element_type=jnp.float32).astype(jnp.bfloat16)
        meta = lax.dot_general(
            slot_bf, pick, (((1,), (1,)), ((), ())), preferred_element_type=jnp.float32
        )[0:1, :]
        if d == 0:
            zbuf[g, h] = rows
            zmeta[d, :, 0:cap] = meta
            zmeta[d, :, 128:256] = jnp.broadcast_to(overflow, (1, 128))
        else:
            zsend[d] = rows
            zmeta_send[d, :, 0:cap] = meta
            zmeta_send[d, :, 128:256] = jnp.broadcast_to(overflow, (1, 128))
            row_copy, meta_copy = z_copies(d)
            meta_copy.start()
            row_copy.start()

    best[...] = jnp.full(best.shape, -1.0, jnp.float32)
    slot_lane = iota((PEERS * 8, cap), 0).astype(jnp.float32)
    flag = jnp.zeros((1, 128), jnp.float32)

    def scatter(g):
        picks = []
        flags = []
        for h, d in enumerate(PAIRS[g]):
            if d:
                row_copy, meta_copy = z_copies(d)
                meta_copy.wait_recv()
                row_copy.wait_recv()
            meta = zmeta[d, :, 0:cap]
            where_to = jnp.where(meta > 0.0, meta - 1.0 + float(4 * h), -1.0)
            picks.append(as_f32(slot_lane == where_to))
            flags.append(zmeta[d, :, 128:256])
        pick = jnp.concatenate(picks, axis=1)
        filled = jnp.sum(pick, axis=1, keepdims=True)
        rows = jnp.dot(
            pick.astype(jnp.bfloat16),
            zbuf[g].reshape(2 * cap, width),
            preferred_element_type=jnp.float32,
        )
        mark = jnp.where(iota((PEERS * 8, 128), 1) == 0, EMPTY * (1.0 - filled), 0.0)
        psend[g, :, :, 0:128] = (rows[:, 0:128] + mark).astype(jnp.bfloat16).reshape(PEERS, 8, 128)
        psend[g, :, :, 128:] = rows[:, 128:].astype(jnp.bfloat16).reshape(PEERS, 8, width - 128)
        local = pltpu.make_async_copy(psend.at[g, my_p], pbuf.at[g, my_p], loc_sem.at[g])
        local.start()

        def send(i, carry):
            peer = lax.rem(my_p + i, PEERS)
            pltpu.make_async_remote_copy(
                src_ref=psend.at[g, peer],
                dst_ref=pbuf.at[g, my_p],
                send_sem=ps_sem.at[g],
                recv_sem=pr_sem.at[g],
                device_id=p_peer(peer),
                device_id_type=MESH,
            ).start()
            return carry

        lax.fori_loop(1, PEERS, send, 0)
        return jnp.maximum(flags[0], flags[1])

    def all_in_plane(src, dst, send_sem, recv_sem):
        return pltpu.make_async_remote_copy(
            src_ref=src,
            dst_ref=dst,
            send_sem=send_sem,
            recv_sem=recv_sem,
            device_id=p_peer(lax.rem(my_p + 1, PEERS)),
            device_id_type=MESH,
        )

    def compare(g):
        pltpu.make_async_copy(psend.at[g, my_p], pbuf.at[g, my_p], loc_sem.at[g]).wait()
        all_in_plane(
            psend.at[g, pl.ds(0, PEERS - 1)],
            pbuf.at[g, pl.ds(0, PEERS - 1)],
            ps_sem.at[g],
            pr_sem.at[g],
        ).wait_recv()
        mine = pbuf[g].reshape(PEERS * 8, width)
        first = mine[:, 0:128].astype(jnp.float32)[:, 0:1]
        bias[g] = jnp.broadcast_to(jnp.where(first > 1.5, FAR, 0.0), (PEERS * 8, 128))

        def block(rows_j, rows_i, bias_j, i, same):
            similar = lax.dot_general(
                rows_j, rows_i, (((1,), (1,)), ((), ())), preferred_element_type=jnp.float32
            )
            similar = similar + jnp.concatenate([bias_j, bias_j], axis=1)
            if same:
                similar = jnp.where(eye, FAR, similar)
            best[i] = jnp.maximum(best[i], jnp.max(similar, axis=0, keepdims=True))

        block(mine, mine, bias[g], g, True)
        for j in range(g):
            other = pbuf[j].reshape(PEERS * 8, width)
            block(other, mine, bias[j], g, False)
            block(mine, other, bias[g], j, False)

    for g in range(GROUPS):
        flag = jnp.maximum(flag, scatter(g))
    for g in range(GROUPS):
        compare(g)

    ret_send[...] = jnp.zeros(ret_send.shape, jnp.float32)
    for half in range(2):
        for g in range(GROUPS):
            ret_send[half, g : g + 1, :] = best[g, :, half * 128 : half * 128 + 128]
        ret_send[half, 4:5, :] = flag
    local = pltpu.make_async_copy(ret_send.at[my_p // 16], ret_buf.at[my_p], loc_sem.at[GROUPS])
    local.start()

    def send_back(i, carry):
        peer = lax.rem(my_p + i, PEERS)
        pltpu.make_async_remote_copy(
            src_ref=ret_send.at[peer // 16],
            dst_ref=ret_buf.at[my_p],
            send_sem=rs_sem,
            recv_sem=rr_sem,
            device_id=p_peer(peer),
            device_id_type=MESH,
        ).start()
        return carry

    lax.fori_loop(1, PEERS, send_back, 0)
    local.wait()
    all_in_plane(
        ret_buf.at[pl.ds(0, PEERS - 1)], ret_buf.at[pl.ds(0, PEERS - 1)], rs_sem, rr_sem
    ).wait()
    came = ret_buf[...]
    flag_ref[...] = jnp.max(came[:, 4, :], axis=0, keepdims=True)
    mine = iota((8, 128), 1) == 8 * lax.rem(my_p, 16) + iota((8, 128), 0)
    back = lax.dot_general(
        as_f32(mine),
        came.reshape(PEERS * 8, 128),
        (((1,), (1,)), ((), ())),
        precision=lax.Precision.HIGHEST,
        preferred_element_type=jnp.float32,
    )
    zret_buf[0] = back
    zret_send[...] = back

    def z_back(d):
        return pltpu.make_async_remote_copy(
            src_ref=zret_send,
            dst_ref=zret_buf.at[d],
            send_sem=zrs_sem.at[d],
            recv_sem=zrr_sem.at[d],
            device_id=z_peer(PLANES - d),
            device_id_type=MESH,
        )

    for d in range(1, PLANES):
        z_back(d).start()

    upper = (rel >= 1) & (rel <= 4)
    group = jnp.where(upper, rel - 1, (PLANES - rel) & 7)
    lane_of = as_f32(peer_of * 8 + group)
    row_of = as_f32(rel * 8 + jnp.where(upper, 4, 0)) + rank
    look = as_f32(sub_i.astype(jnp.float32) == lane_of)
    for d in range(1, PLANES):
        z_back(d).wait_recv()
    found = jnp.dot(
        zret_buf[...].reshape(PLANES * 8, PEERS * 8),
        look,
        precision=lax.Precision.HIGHEST,
        preferred_element_type=jnp.float32,
    )
    right = iota((PLANES * 8, docs), 0).astype(jnp.float32) == row_of
    found = jnp.sum(jnp.where(right, found, 0.0), axis=0, keepdims=True)
    out_ref[...] = jnp.where(valid, jnp.maximum(found, -1.0), -1.0)

    for d in range(1, PLANES):
        row_copy, meta_copy = z_copies(d)
        row_copy.wait_send()
        meta_copy.wait_send()
        z_back(d).wait_send()
    for g in range(GROUPS):
        all_in_plane(
            psend.at[g, pl.ds(0, PEERS - 1)],
            pbuf.at[g, pl.ds(0, PEERS - 1)],
            ps_sem.at[g],
            pr_sem.at[g],
        ).wait_send()


def place(d):
    for g, pair in enumerate(PAIRS):
        if d in pair:
            return g, pair.index(d)


def route(cap, collective_id, embeddings, cluster, valid):
    docs, width = embeddings.shape
    vmem = pl.BlockSpec(memory_space=pltpu.VMEM)
    dma = pltpu.SemaphoreType.DMA
    return pl.pallas_call(
        functools.partial(kernel, cap),
        out_shape=(
            jax.ShapeDtypeStruct((1, docs), jnp.float32),
            jax.ShapeDtypeStruct((1, 128), jnp.float32),
        ),
        in_specs=[pl.BlockSpec(memory_space=pl.ANY)] * 3,
        out_specs=(vmem, vmem),
        scratch_shapes=[
            pltpu.VMEM((docs, width), jnp.bfloat16),
            pltpu.VMEM((1, docs), jnp.int32),
            pltpu.VMEM((1, docs), jnp.int32),
            pltpu.VMEM((PLANES, cap, width), jnp.bfloat16),
            pltpu.VMEM((PLANES, 1, 256), jnp.float32),
            pltpu.VMEM((GROUPS, 2, cap, width), jnp.bfloat16),
            pltpu.VMEM((PLANES, 1, 256), jnp.float32),
            pltpu.VMEM((GROUPS, PEERS, 8, width), jnp.bfloat16),
            pltpu.VMEM((GROUPS, PEERS, 8, width), jnp.bfloat16),
            pltpu.VMEM((GROUPS, PEERS * 8, 128), jnp.float32),
            pltpu.VMEM((GROUPS, 1, PEERS * 8), jnp.float32),
            pltpu.VMEM((2, 8, 128), jnp.float32),
            pltpu.VMEM((PEERS, 8, 128), jnp.float32),
            pltpu.VMEM((8, PEERS * 8), jnp.float32),
            pltpu.VMEM((PLANES, 8, PEERS * 8), jnp.float32),
            dma((PLANES,)),
            dma((PLANES,)),
            dma((PLANES,)),
            dma((PLANES,)),
            dma((GROUPS,)),
            dma((GROUPS,)),
            dma((GROUPS + 1,)),
            dma(()),
            dma(()),
            dma((PLANES,)),
            dma((PLANES,)),
            dma((3,)),
        ],
        compiler_params=pltpu.CompilerParams(
            collective_id=collective_id, has_side_effects=True, vmem_limit_bytes=40 << 20
        ),
        name=f"route_{cap}",
    )(embeddings, cluster, valid)


def per_device(embeddings, doc_cluster, doc_valid):
    docs = embeddings.shape[0]
    args = (embeddings, doc_cluster.reshape(1, docs), doc_valid.reshape(1, docs))
    best, flag = route(CAP, 0, *args)
    best = lax.cond(flag[0, 0] > 0.0, lambda: route(MOST, 1, *args)[0], lambda: best)
    return best.reshape(docs)


def solution(mesh):
    placed = (P(("shard", "blk"), None), P(("shard", "blk")), P(("shard", "blk")))
    return jax.shard_map(
        per_device, mesh=mesh, in_specs=placed, out_specs=P(("shard", "blk")), check_vma=False
    )
```

```python
import functools
import math

import jax
import jax.numpy as jnp
from jax import lax
from jax.experimental import pallas as pl
from jax.experimental.pallas import tpu as pltpu
from jax.sharding import PartitionSpec as P

MESH = pl.DeviceIdType.MESH
PLANES = 8
PEERS = 32
EMPTY = 2.0
FAR = -8.0

CAP = 56
MOST = 128

GROUPS = ((0,), (1, 7), (2, 6), (3, 5), (4,))
ORDER = (1, 7, 0, 2, 6, 3, 5, 4)
PLACE = {d: i for i, d in enumerate(d for group in GROUPS for d in group)}


def iota(shape, dim):
    return lax.broadcasted_iota(jnp.int32, shape, dim)


def as_f32(mask):
    return mask.astype(jnp.float32)


def parts(values):
    high = values.astype(jnp.bfloat16)
    rest = values - high.astype(jnp.float32)
    middle = rest.astype(jnp.bfloat16)
    low = (rest - middle.astype(jnp.float32)).astype(jnp.bfloat16)
    return jnp.concatenate([high, middle, low], axis=0)


def kernel(
    cap,
    emb_hbm,
    clus_hbm,
    valid_hbm,
    out_ref,
    flag_ref,
    clus_out,
    valid_out,
    emb_ref,
    clus_ref,
    valid_ref,
    zsend,
    zmeta_send,
    zbuf,
    zmeta,
    psends,
    pbufs,
    biases,
    bests,
    ret_send,
    ret_buf,
    zret_send,
    zret_buf,
    zs_sem,
    zr_sem,
    zms_sem,
    zmr_sem,
    ps_sem,
    pr_sem,
    loc_sem,
    rs_sem,
    rr_sem,
    zrs_sem,
    zrr_sem,
    in_sem,
):
    docs, width = emb_ref.shape
    shard, blk = lax.axis_index("shard"), lax.axis_index("blk")
    my_z = shard // PLANES
    my_p = lax.rem(shard, PLANES) * 4 + blk

    def at(z, p):
        return (z * PLANES + p // 4, lax.rem(p, 4))

    def z_peer(d):
        return at(lax.rem(my_z + d, PLANES), my_p)

    def p_peer(p):
        return at(my_z, p)

    loads = [
        pltpu.make_async_copy(src, dst, in_sem.at[i])
        for i, (src, dst) in enumerate(
            ((emb_hbm, emb_ref), (clus_hbm, clus_ref), (valid_hbm, valid_ref))
        )
    ]
    for load in loads:
        load.start()

    barrier = pltpu.get_barrier_semaphore()
    for d in range(1, PLANES):
        pl.semaphore_signal(barrier, inc=1, device_id=z_peer(d), device_id_type=MESH)

    def greet(i, carry):
        peer = lax.rem(my_p + i, PEERS)
        pl.semaphore_signal(barrier, inc=1, device_id=p_peer(peer), device_id_type=MESH)
        return carry

    lax.fori_loop(1, PEERS, greet, 0)

    for load in loads[1:]:
        load.wait()
    clus = clus_ref[...]
    valid = valid_ref[...] > 0
    clus_out[...] = clus
    valid_out[...] = valid_ref[...]
    owner, sub = clus & 63, clus >> 6
    plane = ((owner >> 3) + 2 * sub) & (PLANES - 1)
    peer_of = (owner & 7) * 4 + sub
    rel = (plane - my_z + PLANES) & (PLANES - 1)
    rel_row = as_f32(jnp.where(valid, rel, -1))
    key_row = as_f32(jnp.where(valid, clus, -1))
    sub_i, lane_i = iota((docs, docs), 0), iota((docs, docs), 1)
    eye = sub_i == lane_i
    earlier = sub_i < lane_i

    def column(row):
        wide = jnp.broadcast_to(row, (docs, docs))
        return jnp.sum(jnp.where(eye, wide, 0.0), axis=1, keepdims=True)

    key_col, rel_col = column(key_row), column(rel_row)
    rank = jnp.sum(as_f32((key_col == key_row) & earlier), axis=0, keepdims=True)
    rank_z = jnp.sum(as_f32((rel_col == rel_row) & earlier), axis=0, keepdims=True)
    slot = {
        n: jnp.broadcast_to(
            jnp.where(valid, as_f32(peer_of * n) + rank + 1.0, 0.0), (8, docs)
        ).astype(jnp.bfloat16)
        for n in (4, 8)
    }
    fits = valid & (rank_z < float(cap))
    overflow = jnp.max(as_f32(valid & (rank_z >= float(cap))), axis=1, keepdims=True)
    target = jnp.where(fits, rel_row * float(cap) + rank_z, -1.0)

    loads[0].wait()
    values = emb_ref[...].astype(jnp.float32)
    scale = lax.rsqrt(jnp.mean(values * values, axis=1, keepdims=True) + 1e-05) / math.sqrt(width)
    unit = (values * scale).astype(jnp.bfloat16)

    pl.semaphore_wait(barrier, PLANES - 1 + PEERS - 1)

    def z_copies(d):
        rows = pltpu.make_async_remote_copy(
            src_ref=zsend.at[d],
            dst_ref=zbuf.at[PLACE[d]],
            send_sem=zs_sem.at[d],
            recv_sem=zr_sem.at[d],
            device_id=z_peer(d),
            device_id_type=MESH,
        )
        meta = pltpu.make_async_remote_copy(
            src_ref=zmeta_send.at[d],
            dst_ref=zmeta.at[d],
            send_sem=zms_sem.at[d],
            recv_sem=zmr_sem.at[d],
            device_id=z_peer(d),
            device_id_type=MESH,
        )
        return rows, meta

    lane128 = iota((1, 128), 1)
    for d in ORDER:
        pick = iota((cap, docs), 0).astype(jnp.float32) + float(d * cap) == target
        pick = as_f32(pick).astype(jnp.bfloat16)
        rows = jnp.dot(pick, unit, preferred_element_type=jnp.float32).astype(jnp.bfloat16)
        meta = lax.dot_general(
            slot[4 if d in (0, 4) else 8], pick, (((1,), (1,)), ((), ())), preferred_element_type=jnp.float32
        )[0:1, :]
        if d == 0:
            zbuf[PLACE[d]] = rows
            zmeta[d, :, 0:cap] = meta
            zmeta[d, :, 128:256] = jnp.broadcast_to(overflow, (1, 128))
        else:
            zsend[d] = rows
            zmeta_send[d, :, 0:cap] = meta
            zmeta_send[d, :, 128:256] = jnp.broadcast_to(overflow, (1, 128))
            row_copy, meta_copy = z_copies(d)
            if d != 4:
                meta_copy.start()
                row_copy.start()

    for best in bests:
        best[...] = jnp.full(best.shape, -1.0, jnp.float32)
    flag = jnp.zeros((1, 128), jnp.float32)

    def scatter(g):
        picks = []
        flags = []
        psend, pbuf = psends[g], pbufs[g]
        slots = psend.shape[1]
        slot_lane = iota((PEERS * slots, cap), 0).astype(jnp.float32)
        for h, d in enumerate(GROUPS[g]):
            if d:
                row_copy, meta_copy = z_copies(d)
                meta_copy.wait_recv()
                row_copy.wait_recv()
            meta = zmeta[d, :, 0:cap]
            where_to = jnp.where(meta > 0.0, meta - 1.0 + float(4 * h), -1.0)
            picks.append(as_f32(slot_lane == where_to))
            flags.append(zmeta[d, :, 128:256])
        pick = jnp.concatenate(picks, axis=1) if len(picks) > 1 else picks[0]
        filled = jnp.sum(pick, axis=1, keepdims=True)
        rows = jnp.dot(
            pick.astype(jnp.bfloat16),
            zbuf[PLACE[GROUPS[g][0]] : PLACE[GROUPS[g][-1]] + 1].reshape(len(picks) * cap, width),
            preferred_element_type=jnp.float32,
        )
        mark = jnp.where(iota((PEERS * slots, 128), 1) == 0, EMPTY * (1.0 - filled), 0.0)
        head = (rows[:, 0:128] + mark).astype(jnp.bfloat16)
        psend[:, :, 0:128] = head.reshape(PEERS, slots, 128)
        tail = rows[:, 128:].astype(jnp.bfloat16)
        psend[:, :, 128:] = tail.reshape(PEERS, slots, width - 128)
        local = pltpu.make_async_copy(psend.at[my_p], pbuf.at[my_p], loc_sem.at[g])
        local.start()

        def send(i, carry):
            peer = lax.rem(my_p + i, PEERS)
            pltpu.make_async_remote_copy(
                src_ref=psend.at[peer],
                dst_ref=pbuf.at[my_p],
                send_sem=ps_sem.at[g],
                recv_sem=pr_sem.at[g],
                device_id=p_peer(peer),
                device_id_type=MESH,
            ).start()
            return carry

        lax.fori_loop(1, PEERS, send, 0)
        return functools.reduce(jnp.maximum, flags)

    def all_in_plane(src, dst, send_sem, recv_sem):
        return pltpu.make_async_remote_copy(
            src_ref=src,
            dst_ref=dst,
            send_sem=send_sem,
            recv_sem=recv_sem,
            device_id=p_peer(lax.rem(my_p + 1, PEERS)),
            device_id_type=MESH,
        )

    def in_plane(g):
        return all_in_plane(
            psends[g].at[pl.ds(0, PEERS - 1)],
            pbufs[g].at[pl.ds(0, PEERS - 1)],
            ps_sem.at[g],
            pr_sem.at[g],
        )

    def rows_of(g):
        return pbufs[g][...].reshape(-1, width)

    def compare(g):
        pltpu.make_async_copy(psends[g].at[my_p], pbufs[g].at[my_p], loc_sem.at[g]).wait()
        in_plane(g).wait_recv()
        mine = rows_of(g)
        first = mine[:, 0:128].astype(jnp.float32)[:, 0:1]
        biases[g][...] = jnp.broadcast_to(jnp.where(first > 1.5, FAR, 0.0), biases[g].shape)

        def block(rows_j, rows_i, j, i):
            similar = lax.dot_general(
                rows_j, rows_i, (((1,), (1,)), ((), ())), preferred_element_type=jnp.float32
            )
            away = biases[j][...]
            if rows_i.shape[0] > 128:
                away = jnp.concatenate([away, away], axis=1)
            similar = similar + away
            if i == j:
                same = iota(similar.shape, 0) == iota(similar.shape, 1)
                similar = jnp.where(same, FAR, similar)
            bests[i][...] = jnp.maximum(bests[i][...], jnp.max(similar, axis=0, keepdims=True))

        block(mine, mine, g, g)
        for j in range(g):
            other = rows_of(j)
            block(other, mine, j, g)
            block(mine, other, g, j)

    for g in range(len(GROUPS)):
        if g == len(GROUPS) - 1:
            compare(0)
            compare(1)
        if g == 2:
            for copy in z_copies(4):
                copy.start()
        flag = jnp.maximum(flag, scatter(g))
    for g in range(2, len(GROUPS)):
        compare(g)

    ret_send[...] = jnp.zeros(ret_send.shape, jnp.float32)
    for half in range(2):
        for g, best in enumerate(bests):
            first = half * 128 if best.shape[1] > 128 else 0
            ret_send[half, g : g + 1, :] = best[:, first : first + 128]
        ret_send[half, 5:6, :] = flag
    local = pltpu.make_async_copy(ret_send.at[my_p // 16], ret_buf.at[my_p], loc_sem.at[len(GROUPS)])
    local.start()

    def send_back(i, carry):
        peer = lax.rem(my_p + i, PEERS)
        pltpu.make_async_remote_copy(
            src_ref=ret_send.at[peer // 16],
            dst_ref=ret_buf.at[my_p],
            send_sem=rs_sem,
            recv_sem=rr_sem,
            device_id=p_peer(peer),
            device_id_type=MESH,
        ).start()
        return carry

    lax.fori_loop(1, PEERS, send_back, 0)
    number, lane = iota((16, 128), 0), iota((16, 128), 1)
    mine = jnp.where(
        number < 8,
        as_f32(lane == 8 * lax.rem(my_p, 16) + number),
        as_f32((lane == 4 * my_p + number - 8) & (number < 12)),
    ).astype(jnp.bfloat16)
    local.wait()
    all_in_plane(
        ret_buf.at[pl.ds(0, PEERS - 1)], ret_buf.at[pl.ds(0, PEERS - 1)], rs_sem, rr_sem
    ).wait_recv()
    came = ret_buf[...]
    flag_ref[...] = jnp.max(came[:, 5, :], axis=0, keepdims=True)
    back = lax.dot_general(
        mine,
        parts(came.reshape(PEERS * 8, 128)),
        (((1,), (1,)), ((), ())),
        preferred_element_type=jnp.float32,
    )
    back = back[:, 0:256] + back[:, 256:512] + back[:, 512:768]
    group = iota((8, PEERS * 8), 1) & 7
    alone = (group == 0) | (group == len(GROUPS) - 1)
    back = jnp.where(alone, back[8:16], back[0:8])
    zret_buf[0] = back
    zret_send[...] = back

    def z_back(d):
        return pltpu.make_async_remote_copy(
            src_ref=zret_send,
            dst_ref=zret_buf.at[d],
            send_sem=zrs_sem.at[d],
            recv_sem=zrr_sem.at[d],
            device_id=z_peer(PLANES - d),
            device_id_type=MESH,
        )

    for d in range(1, PLANES):
        z_back(d).start()

    upper = rel > 4
    lane_of = as_f32(peer_of * 8 + jnp.where(upper, PLANES - rel, rel))
    row_of = as_f32(rel * 8 + jnp.where(upper, 4, 0)) + rank
    look = as_f32(sub_i.astype(jnp.float32) == lane_of).astype(jnp.bfloat16)
    for d in range(1, PLANES):
        z_back(d).wait_recv()
    found = jnp.dot(
        parts(zret_buf[...].reshape(PLANES * 8, PEERS * 8)),
        look,
        preferred_element_type=jnp.float32,
    )
    found = found[0:64] + found[64:128] + found[128:192]
    right = iota((PLANES * 8, docs), 0).astype(jnp.float32) == row_of
    found = jnp.sum(jnp.where(right, found, 0.0), axis=0, keepdims=True)
    out_ref[...] = jnp.where(valid, jnp.maximum(found, -1.0), -1.0)

    for d in range(1, PLANES):
        row_copy, meta_copy = z_copies(d)
        row_copy.wait_send()
        meta_copy.wait_send()
        z_back(d).wait_send()
    for g in range(len(GROUPS)):
        in_plane(g).wait_send()
    all_in_plane(
        ret_buf.at[pl.ds(0, PEERS - 1)], ret_buf.at[pl.ds(0, PEERS - 1)], rs_sem, rr_sem
    ).wait_send()


def route(cap, collective_id, space, embeddings, cluster, valid):
    docs, width = embeddings.shape
    vmem = pl.BlockSpec(memory_space=pltpu.VMEM)
    dma = pltpu.SemaphoreType.DMA
    slots = [4 * len(group) for group in GROUPS]
    return pl.pallas_call(
        functools.partial(kernel, cap),
        out_shape=(
            jax.ShapeDtypeStruct((1, docs), jnp.float32),
            jax.ShapeDtypeStruct((1, 128), jnp.float32),
            jax.ShapeDtypeStruct((1, docs), jnp.int32),
            jax.ShapeDtypeStruct((1, docs), jnp.int32),
        ),
        in_specs=[pl.BlockSpec(memory_space=space)] * 3,
        out_specs=(vmem,) * 4,
        scratch_shapes=[
            pltpu.VMEM((docs, width), jnp.bfloat16),
            pltpu.VMEM((1, docs), jnp.int32),
            pltpu.VMEM((1, docs), jnp.int32),
            pltpu.VMEM((PLANES, cap, width), jnp.bfloat16),
            pltpu.VMEM((PLANES, 1, 256), jnp.float32),
            pltpu.VMEM((PLANES, cap, width), jnp.bfloat16),
            pltpu.VMEM((PLANES, 1, 256), jnp.float32),
            [pltpu.VMEM((PEERS, n, width), jnp.bfloat16) for n in slots],
            [pltpu.VMEM((PEERS, n, width), jnp.bfloat16) for n in slots],
            [pltpu.VMEM((PEERS * n, 128), jnp.float32) for n in slots],
            [pltpu.VMEM((1, PEERS * n), jnp.float32) for n in slots],
            pltpu.VMEM((2, 8, 128), jnp.float32),
            pltpu.VMEM((PEERS, 8, 128), jnp.float32),
            pltpu.VMEM((8, PEERS * 8), jnp.float32),
            pltpu.VMEM((PLANES, 8, PEERS * 8), jnp.float32),
            dma((PLANES,)),
            dma((PLANES,)),
            dma((PLANES,)),
            dma((PLANES,)),
            dma((len(GROUPS),)),
            dma((len(GROUPS),)),
            dma((len(GROUPS) + 1,)),
            dma(()),
            dma(()),
            dma((PLANES,)),
            dma((PLANES,)),
            dma((3,)),
        ],
        compiler_params=pltpu.CompilerParams(
            collective_id=collective_id, has_side_effects=True, vmem_limit_bytes=40 << 20
        ),
        name=f"route_{cap}",
    )(embeddings, cluster, valid)


def per_device(embeddings, doc_cluster, doc_valid):
    docs = embeddings.shape[0]
    cluster, valid = doc_cluster.reshape(1, docs), doc_valid.reshape(1, docs)
    hbm = [pltpu.with_memory_space_constraint(a, pltpu.HBM) for a in (embeddings, cluster, valid)]
    best, flag, cluster, valid = route(CAP, 0, pltpu.HBM, *hbm)
    best = lax.cond(
        flag[0, 0] > 0.0,
        lambda: route(MOST, 1, pl.ANY, embeddings, cluster, valid)[0],
        lambda: best,
    )
    return best.reshape(docs)


def solution(mesh):
    placed = (P(("shard", "blk"), None), P(("shard", "blk")), P(("shard", "blk")))
    return jax.shard_map(
        per_device, mesh=mesh, in_specs=placed, out_specs=P(("shard", "blk")), check_vma=False
    )
```

```python
import functools
import math

import jax
import jax.numpy as jnp
from jax import lax
from jax.experimental import pallas as pl
from jax.experimental.pallas import tpu as pltpu
from jax.sharding import PartitionSpec as P

MESH = pl.DeviceIdType.MESH
PLANES = 8
PEERS = 32
EMPTY = 2.0
FAR = -8.0

CAP = 56
MOST = 128

STEPS = sorted(
    ((x, y, core) for x in range(4) for y in range(4) for core in range(2) if (x, y, core) != (0, 0, 0)),
    key=lambda step: (-min(step[0], 4 - step[0]) - min(step[1], 4 - step[1]), step),
)
GROUPS = ((0,), (1, 7), (2, 6), (3, 5), (4,))
ORDER = (1, 7, 0, 2, 6, 3, 5, 4)
PLACE = {d: i for i, d in enumerate(d for group in GROUPS for d in group)}


def iota(shape, dim):
    return lax.broadcasted_iota(jnp.int32, shape, dim)


def as_f32(mask):
    return mask.astype(jnp.float32)


def parts(values):
    high = values.astype(jnp.bfloat16)
    rest = values - high.astype(jnp.float32)
    middle = rest.astype(jnp.bfloat16)
    low = (rest - middle.astype(jnp.float32)).astype(jnp.bfloat16)
    return jnp.concatenate([high, middle, low], axis=0)


def kernel(
    cap,
    emb_hbm,
    clus_hbm,
    valid_hbm,
    out_ref,
    flag_ref,
    clus_out,
    valid_out,
    emb_ref,
    clus_ref,
    valid_ref,
    zsend,
    zmeta_send,
    zbuf,
    zmeta,
    psends,
    pbufs,
    biases,
    bests,
    ret_send,
    ret_buf,
    zret_send,
    zret_buf,
    zs_sem,
    zr_sem,
    zms_sem,
    zmr_sem,
    ps_sem,
    pr_sem,
    loc_sem,
    rs_sem,
    rr_sem,
    zrs_sem,
    zrr_sem,
    in_sem,
):
    docs, width = emb_ref.shape
    shard, blk = lax.axis_index("shard"), lax.axis_index("blk")
    my_z = shard // PLANES
    my_p = lax.rem(shard, PLANES) * 4 + blk

    def at(z, p):
        return (z * PLANES + p // 4, lax.rem(p, 4))

    def z_peer(d):
        return at(lax.rem(my_z + d, PLANES), my_p)

    def p_peer(p):
        return at(my_z, p)

    loads = [
        pltpu.make_async_copy(src, dst, in_sem.at[i])
        for i, (src, dst) in enumerate(
            ((emb_hbm, emb_ref), (clus_hbm, clus_ref), (valid_hbm, valid_ref))
        )
    ]
    for load in loads:
        load.start()

    my_x = lax.rem(my_p // 2, 2) * 2 + my_p // 16
    my_y, my_core = lax.rem(my_p // 4, 4), lax.rem(my_p, 2)

    def stepped(step):
        x = lax.rem(my_x + step[0], 4)
        y = lax.rem(my_y + step[1], 4)
        return lax.rem(x, 2) * 16 + y * 4 + (x // 2) * 2 + lax.rem(my_core + step[2], 2)

    barrier = pltpu.get_barrier_semaphore()
    for d in range(1, PLANES):
        pl.semaphore_signal(barrier, inc=1, device_id=z_peer(d), device_id_type=MESH)

    def greet(i, carry):
        peer = lax.rem(my_p + i, PEERS)
        pl.semaphore_signal(barrier, inc=1, device_id=p_peer(peer), device_id_type=MESH)
        return carry

    lax.fori_loop(1, PEERS, greet, 0)

    for load in loads[1:]:
        load.wait()
    clus = clus_ref[...]
    valid = valid_ref[...] > 0
    clus_out[...] = clus
    valid_out[...] = valid_ref[...]
    owner, sub = clus & 63, clus >> 6
    plane = ((owner >> 3) + 2 * sub) & (PLANES - 1)
    peer_of = (owner & 7) * 4 + sub
    rel = (plane - my_z + PLANES) & (PLANES - 1)
    rel_row = as_f32(jnp.where(valid, rel, -1))
    key_row = as_f32(jnp.where(valid, clus, -1))
    sub_i, lane_i = iota((docs, docs), 0), iota((docs, docs), 1)
    eye = sub_i == lane_i
    earlier = sub_i < lane_i

    def column(row):
        wide = jnp.broadcast_to(row, (docs, docs))
        return jnp.sum(jnp.where(eye, wide, 0.0), axis=1, keepdims=True)

    key_col, rel_col = column(key_row), column(rel_row)
    rank = jnp.sum(as_f32((key_col == key_row) & earlier), axis=0, keepdims=True)
    rank_z = jnp.sum(as_f32((rel_col == rel_row) & earlier), axis=0, keepdims=True)
    slot = {
        n: jnp.broadcast_to(
            jnp.where(valid, as_f32(peer_of * n) + rank + 1.0, 0.0), (8, docs)
        ).astype(jnp.bfloat16)
        for n in (4, 8)
    }
    fits = valid & (rank_z < float(cap))
    overflow = jnp.max(as_f32(valid & (rank_z >= float(cap))), axis=1, keepdims=True)
    target = jnp.where(fits, rel_row * float(cap) + rank_z, -1.0)

    loads[0].wait()
    values = emb_ref[...].astype(jnp.float32)
    scale = lax.rsqrt(jnp.mean(values * values, axis=1, keepdims=True) + 1e-05) / math.sqrt(width)
    unit = (values * scale).astype(jnp.bfloat16)

    pl.semaphore_wait(barrier, PLANES - 1 + PEERS - 1)

    def z_copies(d):
        rows = pltpu.make_async_remote_copy(
            src_ref=zsend.at[d],
            dst_ref=zbuf.at[PLACE[d]],
            send_sem=zs_sem.at[d],
            recv_sem=zr_sem.at[d],
            device_id=z_peer(d),
            device_id_type=MESH,
        )
        meta = pltpu.make_async_remote_copy(
            src_ref=zmeta_send.at[d],
            dst_ref=zmeta.at[d],
            send_sem=zms_sem.at[d],
            recv_sem=zmr_sem.at[d],
            device_id=z_peer(d),
            device_id_type=MESH,
        )
        return rows, meta

    lane128 = iota((1, 128), 1)
    for d in ORDER:
        pick = iota((cap, docs), 0).astype(jnp.float32) + float(d * cap) == target
        pick = as_f32(pick).astype(jnp.bfloat16)
        rows = jnp.dot(pick, unit, preferred_element_type=jnp.float32).astype(jnp.bfloat16)
        meta = lax.dot_general(
            slot[4 if d in (0, 4) else 8], pick, (((1,), (1,)), ((), ())), preferred_element_type=jnp.float32
        )[0:1, :]
        if d == 0:
            zbuf[PLACE[d]] = rows
            zmeta[d, :, 0:cap] = meta
            zmeta[d, :, 128:256] = jnp.broadcast_to(overflow, (1, 128))
        else:
            zsend[d] = rows
            zmeta_send[d, :, 0:cap] = meta
            zmeta_send[d, :, 128:256] = jnp.broadcast_to(overflow, (1, 128))
            row_copy, meta_copy = z_copies(d)
            if d != 4:
                meta_copy.start()
                row_copy.start()

    for best in bests:
        best[...] = jnp.full(best.shape, -1.0, jnp.float32)
    flag = jnp.zeros((1, 128), jnp.float32)

    def scatter(g):
        picks = []
        flags = []
        psend, pbuf = psends[g], pbufs[g]
        slots = psend.shape[1]
        slot_lane = iota((PEERS * slots, cap), 0).astype(jnp.float32)
        for h, d in enumerate(GROUPS[g]):
            if d:
                row_copy, meta_copy = z_copies(d)
                meta_copy.wait_recv()
                row_copy.wait_recv()
            meta = zmeta[d, :, 0:cap]
            where_to = jnp.where(meta > 0.0, meta - 1.0 + float(4 * h), -1.0)
            picks.append(as_f32(slot_lane == where_to))
            flags.append(zmeta[d, :, 128:256])
        pick = jnp.concatenate(picks, axis=1) if len(picks) > 1 else picks[0]
        filled = jnp.sum(pick, axis=1, keepdims=True)
        rows = jnp.dot(
            pick.astype(jnp.bfloat16),
            zbuf[PLACE[GROUPS[g][0]] : PLACE[GROUPS[g][-1]] + 1].reshape(len(picks) * cap, width),
            preferred_element_type=jnp.float32,
        )
        mark = jnp.where(iota((PEERS * slots, 128), 1) == 0, EMPTY * (1.0 - filled), 0.0)
        head = (rows[:, 0:128] + mark).astype(jnp.bfloat16)
        psend[:, :, 0:128] = head.reshape(PEERS, slots, 128)
        tail = rows[:, 128:].astype(jnp.bfloat16)
        psend[:, :, 128:] = tail.reshape(PEERS, slots, width - 128)
        local = pltpu.make_async_copy(psend.at[my_p], pbuf.at[my_p], loc_sem.at[g])
        local.start()

        def send(i, carry):
            peer = lax.rem(my_p + i, PEERS)
            pltpu.make_async_remote_copy(
                src_ref=psend.at[peer],
                dst_ref=pbuf.at[my_p],
                send_sem=ps_sem.at[g],
                recv_sem=pr_sem.at[g],
                device_id=p_peer(peer),
                device_id_type=MESH,
            ).start()
            return carry

        lax.fori_loop(1, PEERS, send, 0)
        return functools.reduce(jnp.maximum, flags)

    def all_in_plane(src, dst, send_sem, recv_sem):
        return pltpu.make_async_remote_copy(
            src_ref=src,
            dst_ref=dst,
            send_sem=send_sem,
            recv_sem=recv_sem,
            device_id=p_peer(lax.rem(my_p + 1, PEERS)),
            device_id_type=MESH,
        )

    def in_plane(g):
        return all_in_plane(
            psends[g].at[pl.ds(0, PEERS - 1)],
            pbufs[g].at[pl.ds(0, PEERS - 1)],
            ps_sem.at[g],
            pr_sem.at[g],
        )

    def rows_of(g):
        return pbufs[g][...].reshape(-1, width)

    def compare(g):
        pltpu.make_async_copy(psends[g].at[my_p], pbufs[g].at[my_p], loc_sem.at[g]).wait()
        in_plane(g).wait_recv()
        mine = rows_of(g)
        first = mine[:, 0:128].astype(jnp.float32)[:, 0:1]
        biases[g][...] = jnp.broadcast_to(jnp.where(first > 1.5, FAR, 0.0), biases[g].shape)

        def block(rows_j, rows_i, j, i):
            similar = lax.dot_general(
                rows_j, rows_i, (((1,), (1,)), ((), ())), preferred_element_type=jnp.float32
            )
            away = biases[j][...]
            if rows_i.shape[0] > 128:
                away = jnp.concatenate([away, away], axis=1)
            similar = similar + away
            if i == j:
                same = iota(similar.shape, 0) == iota(similar.shape, 1)
                similar = jnp.where(same, FAR, similar)
            bests[i][...] = jnp.maximum(bests[i][...], jnp.max(similar, axis=0, keepdims=True))

        block(mine, mine, g, g)
        for j in range(g):
            other = rows_of(j)
            block(other, mine, j, g)
            block(mine, other, g, j)

    for g in range(len(GROUPS)):
        if g == len(GROUPS) - 1:
            compare(0)
            compare(1)
        if g == 2:
            for copy in z_copies(4):
                copy.start()
        flag = jnp.maximum(flag, scatter(g))
    for g in range(2, len(GROUPS)):
        compare(g)

    ret_send[...] = jnp.zeros(ret_send.shape, jnp.float32)
    for half in range(2):
        for g, best in enumerate(bests):
            first = half * 128 if best.shape[1] > 128 else 0
            ret_send[half, g : g + 1, :] = best[:, first : first + 128]
        ret_send[half, 5:6, :] = flag
    local = pltpu.make_async_copy(ret_send.at[my_p // 16], ret_buf.at[my_p], loc_sem.at[len(GROUPS)])
    local.start()

    for step in STEPS:
        peer = stepped(step)
        pltpu.make_async_remote_copy(
            src_ref=ret_send.at[peer // 16],
            dst_ref=ret_buf.at[my_p],
            send_sem=rs_sem,
            recv_sem=rr_sem,
            device_id=p_peer(peer),
            device_id_type=MESH,
        ).start()
    number, lane = iota((16, 128), 0), iota((16, 128), 1)
    mine = jnp.where(
        number < 8,
        as_f32(lane == 8 * lax.rem(my_p, 16) + number),
        as_f32((lane == 4 * my_p + number - 8) & (number < 12)),
    ).astype(jnp.bfloat16)
    local.wait()
    all_in_plane(
        ret_buf.at[pl.ds(0, PEERS - 1)], ret_buf.at[pl.ds(0, PEERS - 1)], rs_sem, rr_sem
    ).wait_recv()
    came = ret_buf[...]
    flag_ref[...] = jnp.max(came[:, 5, :], axis=0, keepdims=True)
    back = lax.dot_general(
        mine,
        parts(came.reshape(PEERS * 8, 128)),
        (((1,), (1,)), ((), ())),
        preferred_element_type=jnp.float32,
    )
    back = back[:, 0:256] + back[:, 256:512] + back[:, 512:768]
    group = iota((8, PEERS * 8), 1) & 7
    alone = (group == 0) | (group == len(GROUPS) - 1)
    back = jnp.where(alone, back[8:16], back[0:8])
    zret_buf[0] = back
    zret_send[...] = back

    def z_back(d):
        return pltpu.make_async_remote_copy(
            src_ref=zret_send,
            dst_ref=zret_buf.at[d],
            send_sem=zrs_sem.at[d],
            recv_sem=zrr_sem.at[d],
            device_id=z_peer(PLANES - d),
            device_id_type=MESH,
        )

    for d in (4, 3, 5, 2, 6, 1, 7):
        z_back(d).start()

    upper = rel > 4
    lane_of = as_f32(peer_of * 8 + jnp.where(upper, PLANES - rel, rel))
    row_of = as_f32(rel * 8 + jnp.where(upper, 4, 0)) + rank
    look = as_f32(sub_i.astype(jnp.float32) == lane_of).astype(jnp.bfloat16)
    for d in range(1, PLANES):
        z_back(d).wait_recv()
    found = jnp.dot(
        parts(zret_buf[...].reshape(PLANES * 8, PEERS * 8)),
        look,
        preferred_element_type=jnp.float32,
    )
    found = found[0:64] + found[64:128] + found[128:192]
    right = iota((PLANES * 8, docs), 0).astype(jnp.float32) == row_of
    found = jnp.sum(jnp.where(right, found, 0.0), axis=0, keepdims=True)
    out_ref[...] = jnp.where(valid, jnp.maximum(found, -1.0), -1.0)

    for d in range(1, PLANES):
        row_copy, meta_copy = z_copies(d)
        row_copy.wait_send()
        meta_copy.wait_send()
        z_back(d).wait_send()
    for g in range(len(GROUPS)):
        in_plane(g).wait_send()
    all_in_plane(
        ret_buf.at[pl.ds(0, PEERS - 1)], ret_buf.at[pl.ds(0, PEERS - 1)], rs_sem, rr_sem
    ).wait_send()


def route(cap, collective_id, space, embeddings, cluster, valid):
    docs, width = embeddings.shape
    vmem = pl.BlockSpec(memory_space=pltpu.VMEM)
    dma = pltpu.SemaphoreType.DMA
    slots = [4 * len(group) for group in GROUPS]
    return pl.pallas_call(
        functools.partial(kernel, cap),
        out_shape=(
            jax.ShapeDtypeStruct((1, docs), jnp.float32),
            jax.ShapeDtypeStruct((1, 128), jnp.float32),
            jax.ShapeDtypeStruct((1, docs), jnp.int32),
            jax.ShapeDtypeStruct((1, docs), jnp.int32),
        ),
        in_specs=[pl.BlockSpec(memory_space=space)] * 3,
        out_specs=(vmem,) * 4,
        scratch_shapes=[
            pltpu.VMEM((docs, width), jnp.bfloat16),
            pltpu.VMEM((1, docs), jnp.int32),
            pltpu.VMEM((1, docs), jnp.int32),
            pltpu.VMEM((PLANES, cap, width), jnp.bfloat16),
            pltpu.VMEM((PLANES, 1, 256), jnp.float32),
            pltpu.VMEM((PLANES, cap, width), jnp.bfloat16),
            pltpu.VMEM((PLANES, 1, 256), jnp.float32),
            [pltpu.VMEM((PEERS, n, width), jnp.bfloat16) for n in slots],
            [pltpu.VMEM((PEERS, n, width), jnp.bfloat16) for n in slots],
            [pltpu.VMEM((PEERS * n, 128), jnp.float32) for n in slots],
            [pltpu.VMEM((1, PEERS * n), jnp.float32) for n in slots],
            pltpu.VMEM((2, 8, 128), jnp.float32),
            pltpu.VMEM((PEERS, 8, 128), jnp.float32),
            pltpu.VMEM((8, PEERS * 8), jnp.float32),
            pltpu.VMEM((PLANES, 8, PEERS * 8), jnp.float32),
            dma((PLANES,)),
            dma((PLANES,)),
            dma((PLANES,)),
            dma((PLANES,)),
            dma((len(GROUPS),)),
            dma((len(GROUPS),)),
            dma((len(GROUPS) + 1,)),
            dma(()),
            dma(()),
            dma((PLANES,)),
            dma((PLANES,)),
            dma((3,)),
        ],
        compiler_params=pltpu.CompilerParams(
            collective_id=collective_id, has_side_effects=True, vmem_limit_bytes=40 << 20
        ),
        name=f"route_{cap}",
    )(embeddings, cluster, valid)


def per_device(embeddings, doc_cluster, doc_valid):
    docs = embeddings.shape[0]
    cluster, valid = doc_cluster.reshape(1, docs), doc_valid.reshape(1, docs)
    hbm = [pltpu.with_memory_space_constraint(a, pltpu.HBM) for a in (embeddings, cluster, valid)]
    best, flag, cluster, valid = route(CAP, 0, pltpu.HBM, *hbm)
    best = lax.cond(
        flag[0, 0] > 0.0,
        lambda: route(MOST, 1, pl.ANY, embeddings, cluster, valid)[0],
        lambda: best,
    )
    return best.reshape(docs)


def solution(mesh):
    placed = (P(("shard", "blk"), None), P(("shard", "blk")), P(("shard", "blk")))
    return jax.shard_map(
        per_device, mesh=mesh, in_specs=placed, out_specs=P(("shard", "blk")), check_vma=False
    )
```

```python
import functools
import math

import jax
import jax.numpy as jnp
from jax import lax
from jax.experimental import pallas as pl
from jax.experimental.pallas import tpu as pltpu
from jax.sharding import PartitionSpec as P

MESH = pl.DeviceIdType.MESH
PLANES = 8
PEERS = 32
EMPTY = 2.0
FAR = -8.0

CAP = 52
MOST = 128

STEPS = sorted(
    ((x, y, core) for x in range(4) for y in range(4) for core in range(2) if (x, y, core) != (0, 0, 0)),
    key=lambda step: (-min(step[0], 4 - step[0]) - min(step[1], 4 - step[1]), step),
)
GROUPS = ((0,), (1, 7), (2, 6), (3, 5), (4,))
ORDER = (1, 7, 0, 2, 6, 3, 5, 4)
PLACE = {d: i for i, d in enumerate(d for group in GROUPS for d in group)}


def iota(shape, dim):
    return lax.broadcasted_iota(jnp.int32, shape, dim)


def as_f32(mask):
    return mask.astype(jnp.float32)


def parts(values):
    high = values.astype(jnp.bfloat16)
    rest = values - high.astype(jnp.float32)
    middle = rest.astype(jnp.bfloat16)
    low = (rest - middle.astype(jnp.float32)).astype(jnp.bfloat16)
    return jnp.concatenate([high, middle, low], axis=0)


def kernel(
    cap,
    emb_hbm,
    clus_hbm,
    valid_hbm,
    out_ref,
    flag_ref,
    clus_out,
    valid_out,
    emb_ref,
    clus_ref,
    valid_ref,
    zsend,
    zmeta_send,
    zbuf,
    zmeta,
    psends,
    pbufs,
    biases,
    bests,
    ret_send,
    ret_buf,
    zret_send,
    zret_buf,
    zs_sem,
    zr_sem,
    zms_sem,
    zmr_sem,
    ps_sem,
    pr_sem,
    loc_sem,
    rs_sem,
    rr_sem,
    zrs_sem,
    zrr_sem,
    in_sem,
):
    docs, width = emb_ref.shape
    shard, blk = lax.axis_index("shard"), lax.axis_index("blk")
    my_z = shard // PLANES
    my_p = lax.rem(shard, PLANES) * 4 + blk

    def at(z, p):
        return (z * PLANES + p // 4, lax.rem(p, 4))

    def z_peer(d):
        return at(lax.rem(my_z + d, PLANES), my_p)

    def p_peer(p):
        return at(my_z, p)

    loads = [
        pltpu.make_async_copy(src, dst, in_sem.at[i])
        for i, (src, dst) in enumerate(
            ((emb_hbm, emb_ref), (clus_hbm, clus_ref), (valid_hbm, valid_ref))
        )
    ]
    for load in loads:
        load.start()

    my_x = lax.rem(my_p // 2, 2) * 2 + my_p // 16
    my_y, my_core = lax.rem(my_p // 4, 4), lax.rem(my_p, 2)

    def stepped(step):
        x = lax.rem(my_x + step[0], 4)
        y = lax.rem(my_y + step[1], 4)
        return lax.rem(x, 2) * 16 + y * 4 + (x // 2) * 2 + lax.rem(my_core + step[2], 2)

    barrier = pltpu.get_barrier_semaphore()
    for d in (4, 3, 5, 2, 6, 1, 7):
        pl.semaphore_signal(barrier, inc=1, device_id=z_peer(d), device_id_type=MESH)

    for step in STEPS:
        pl.semaphore_signal(
            barrier, inc=1, device_id=p_peer(stepped(step)), device_id_type=MESH
        )

    for load in loads[1:]:
        load.wait()
    clus = clus_ref[...]
    valid = valid_ref[...] > 0
    clus_out[...] = clus
    valid_out[...] = valid_ref[...]
    owner, sub = clus & 63, clus >> 6
    plane = ((owner >> 3) + 2 * sub) & (PLANES - 1)
    peer_of = (owner & 7) * 4 + sub
    rel = (plane - my_z + PLANES) & (PLANES - 1)
    rel_row = as_f32(jnp.where(valid, rel, -1))
    key_row = as_f32(jnp.where(valid, clus, -1))
    sub_i, lane_i = iota((docs, docs), 0), iota((docs, docs), 1)
    eye = sub_i == lane_i
    earlier = sub_i < lane_i

    def column(row):
        wide = jnp.broadcast_to(row, (docs, docs))
        return jnp.sum(jnp.where(eye, wide, 0.0), axis=1, keepdims=True)

    key_col, rel_col = column(key_row), column(rel_row)
    rank = jnp.sum(as_f32((key_col == key_row) & earlier), axis=0, keepdims=True)
    rank_z = jnp.sum(as_f32((rel_col == rel_row) & earlier), axis=0, keepdims=True)
    slot = {
        n: jnp.broadcast_to(
            jnp.where(valid, as_f32(peer_of * n) + rank + 1.0, 0.0), (8, docs)
        ).astype(jnp.bfloat16)
        for n in (4, 8)
    }
    fits = valid & (rank_z < float(cap))
    overflow = jnp.max(as_f32(valid & (rank_z >= float(cap))), axis=1, keepdims=True)
    target = jnp.where(fits, rel_row * float(cap) + rank_z, -1.0)

    loads[0].wait()
    values = emb_ref[...].astype(jnp.float32)
    scale = lax.rsqrt(jnp.mean(values * values, axis=1, keepdims=True) + 1e-05) / math.sqrt(width)
    unit = (values * scale).astype(jnp.bfloat16)

    pl.semaphore_wait(barrier, PLANES - 1 + PEERS - 1)

    def z_copies(d):
        rows = pltpu.make_async_remote_copy(
            src_ref=zsend.at[d],
            dst_ref=zbuf.at[PLACE[d]],
            send_sem=zs_sem.at[d],
            recv_sem=zr_sem.at[d],
            device_id=z_peer(d),
            device_id_type=MESH,
        )
        meta = pltpu.make_async_remote_copy(
            src_ref=zmeta_send.at[d],
            dst_ref=zmeta.at[d],
            send_sem=zms_sem.at[d],
            recv_sem=zmr_sem.at[d],
            device_id=z_peer(d),
            device_id_type=MESH,
        )
        return rows, meta

    lane128 = iota((1, 128), 1)
    for d in ORDER:
        pick = iota((cap, docs), 0).astype(jnp.float32) + float(d * cap) == target
        pick = as_f32(pick).astype(jnp.bfloat16)
        rows = jnp.dot(pick, unit, preferred_element_type=jnp.float32).astype(jnp.bfloat16)
        meta = lax.dot_general(
            slot[4 if d in (0, 4) else 8], pick, (((1,), (1,)), ((), ())), preferred_element_type=jnp.float32
        )[0:1, :]
        if d == 0:
            zbuf[PLACE[d]] = rows.reshape(cap // 4, 4, width)
            zmeta[d, :, 0:cap] = meta
            zmeta[d, :, 128:256] = jnp.broadcast_to(overflow, (1, 128))
        else:
            zsend[d] = rows.reshape(cap // 4, 4, width)
            zmeta_send[d, :, 0:cap] = meta
            zmeta_send[d, :, 128:256] = jnp.broadcast_to(overflow, (1, 128))
            row_copy, meta_copy = z_copies(d)
            if d != 4:
                meta_copy.start()
                row_copy.start()

    for best in bests:
        best[...] = jnp.full(best.shape, -1.0, jnp.float32)
    flag = jnp.zeros((1, 128), jnp.float32)

    def scatter(g):
        picks = []
        flags = []
        psend, pbuf = psends[g], pbufs[g]
        slots = psend.shape[1]
        slot_lane = iota((PEERS * slots, cap), 0).astype(jnp.float32)
        for h, d in enumerate(GROUPS[g]):
            if d:
                row_copy, meta_copy = z_copies(d)
                meta_copy.wait_recv()
                row_copy.wait_recv()
            meta = zmeta[d, :, 0:cap]
            where_to = jnp.where(meta > 0.0, meta - 1.0 + float(4 * h), -1.0)
            picks.append(as_f32(slot_lane == where_to))
            flags.append(zmeta[d, :, 128:256])
        pick = jnp.concatenate(picks, axis=1) if len(picks) > 1 else picks[0]
        filled = jnp.sum(pick, axis=1, keepdims=True)
        rows = jnp.dot(
            pick.astype(jnp.bfloat16),
            zbuf[PLACE[GROUPS[g][0]] : PLACE[GROUPS[g][-1]] + 1].reshape(len(picks) * cap, width),
            preferred_element_type=jnp.float32,
        )
        mark = jnp.where(iota((PEERS * slots, 128), 1) == 0, EMPTY * (1.0 - filled), 0.0)
        head = (rows[:, 0:128] + mark).astype(jnp.bfloat16)
        psend[:, :, 0:128] = head.reshape(PEERS, slots, 128)
        tail = rows[:, 128:].astype(jnp.bfloat16)
        psend[:, :, 128:] = tail.reshape(PEERS, slots, width - 128)
        local = pltpu.make_async_copy(psend.at[my_p], pbuf.at[my_p], loc_sem.at[g])
        local.start()

        def send(i, carry):
            peer = lax.rem(my_p + i, PEERS)
            pltpu.make_async_remote_copy(
                src_ref=psend.at[peer],
                dst_ref=pbuf.at[my_p],
                send_sem=ps_sem.at[g],
                recv_sem=pr_sem.at[g],
                device_id=p_peer(peer),
                device_id_type=MESH,
            ).start()
            return carry

        lax.fori_loop(1, PEERS, send, 0)
        return functools.reduce(jnp.maximum, flags)

    def all_in_plane(src, dst, send_sem, recv_sem):
        return pltpu.make_async_remote_copy(
            src_ref=src,
            dst_ref=dst,
            send_sem=send_sem,
            recv_sem=recv_sem,
            device_id=p_peer(lax.rem(my_p + 1, PEERS)),
            device_id_type=MESH,
        )

    def in_plane(g):
        return all_in_plane(
            psends[g].at[pl.ds(0, PEERS - 1)],
            pbufs[g].at[pl.ds(0, PEERS - 1)],
            ps_sem.at[g],
            pr_sem.at[g],
        )

    def rows_of(g):
        return pbufs[g][...].reshape(-1, width)

    def compare(g):
        pltpu.make_async_copy(psends[g].at[my_p], pbufs[g].at[my_p], loc_sem.at[g]).wait()
        in_plane(g).wait_recv()
        mine = rows_of(g)
        first = mine[:, 0:128].astype(jnp.float32)[:, 0:1]
        biases[g][...] = jnp.broadcast_to(jnp.where(first > 1.5, FAR, 0.0), biases[g].shape)

        def block(rows_j, rows_i, j, i):
            similar = lax.dot_general(
                rows_j, rows_i, (((1,), (1,)), ((), ())), preferred_element_type=jnp.float32
            )
            away = biases[j][...]
            if rows_i.shape[0] > 128:
                away = jnp.concatenate([away, away], axis=1)
            similar = similar + away
            if i == j:
                same = iota(similar.shape, 0) == iota(similar.shape, 1)
                similar = jnp.where(same, FAR, similar)
            bests[i][...] = jnp.maximum(bests[i][...], jnp.max(similar, axis=0, keepdims=True))

        block(mine, mine, g, g)
        for j in range(g):
            other = rows_of(j)
            block(other, mine, j, g)
            block(mine, other, g, j)

    for g in range(len(GROUPS)):
        if g == len(GROUPS) - 1:
            compare(0)
            compare(1)
        if g == 2:
            for copy in z_copies(4):
                copy.start()
        flag = jnp.maximum(flag, scatter(g))
    for g in range(2, len(GROUPS)):
        compare(g)

    ret_send[...] = jnp.zeros(ret_send.shape, jnp.float32)
    for half in range(2):
        for g, best in enumerate(bests):
            first = half * 128 if best.shape[1] > 128 else 0
            ret_send[half, g : g + 1, :] = best[:, first : first + 128]
        ret_send[half, 5:6, :] = flag
    local = pltpu.make_async_copy(ret_send.at[my_p // 16], ret_buf.at[my_p], loc_sem.at[len(GROUPS)])
    local.start()

    for step in STEPS:
        peer = stepped(step)
        pltpu.make_async_remote_copy(
            src_ref=ret_send.at[peer // 16],
            dst_ref=ret_buf.at[my_p],
            send_sem=rs_sem,
            recv_sem=rr_sem,
            device_id=p_peer(peer),
            device_id_type=MESH,
        ).start()
    number, lane = iota((16, 128), 0), iota((16, 128), 1)
    mine = jnp.where(
        number < 8,
        as_f32(lane == 8 * lax.rem(my_p, 16) + number),
        as_f32((lane == 4 * my_p + number - 8) & (number < 12)),
    ).astype(jnp.bfloat16)
    local.wait()
    all_in_plane(
        ret_buf.at[pl.ds(0, PEERS - 1)], ret_buf.at[pl.ds(0, PEERS - 1)], rs_sem, rr_sem
    ).wait_recv()
    came = ret_buf[...]
    flag_ref[...] = jnp.max(came[:, 5, :], axis=0, keepdims=True)
    back = lax.dot_general(
        mine,
        parts(came.reshape(PEERS * 8, 128)),
        (((1,), (1,)), ((), ())),
        preferred_element_type=jnp.float32,
    )
    back = back[:, 0:256] + back[:, 256:512] + back[:, 512:768]
    group = iota((8, PEERS * 8), 1) & 7
    alone = (group == 0) | (group == len(GROUPS) - 1)
    back = jnp.where(alone, back[8:16], back[0:8])
    zret_buf[0] = back
    zret_send[...] = back

    def z_back(d):
        return pltpu.make_async_remote_copy(
            src_ref=zret_send,
            dst_ref=zret_buf.at[d],
            send_sem=zrs_sem.at[d],
            recv_sem=zrr_sem.at[d],
            device_id=z_peer(PLANES - d),
            device_id_type=MESH,
        )

    for d in (4, 3, 5, 2, 6, 1, 7):
        z_back(d).start()

    upper = rel > 4
    lane_of = as_f32(peer_of * 8 + jnp.where(upper, PLANES - rel, rel))
    row_of = as_f32(rel * 8 + jnp.where(upper, 4, 0)) + rank
    look = as_f32(sub_i.astype(jnp.float32) == lane_of).astype(jnp.bfloat16)
    for d in range(1, PLANES):
        z_back(d).wait_recv()
    found = jnp.dot(
        parts(zret_buf[...].reshape(PLANES * 8, PEERS * 8)),
        look,
        preferred_element_type=jnp.float32,
    )
    found = found[0:64] + found[64:128] + found[128:192]
    right = iota((PLANES * 8, docs), 0).astype(jnp.float32) == row_of
    found = jnp.sum(jnp.where(right, found, 0.0), axis=0, keepdims=True)
    out_ref[...] = jnp.where(valid, jnp.maximum(found, -1.0), -1.0)

    for d in range(1, PLANES):
        row_copy, meta_copy = z_copies(d)
        row_copy.wait_send()
        meta_copy.wait_send()
        z_back(d).wait_send()
    for g in range(len(GROUPS)):
        in_plane(g).wait_send()
    all_in_plane(
        ret_buf.at[pl.ds(0, PEERS - 1)], ret_buf.at[pl.ds(0, PEERS - 1)], rs_sem, rr_sem
    ).wait_send()


def route(cap, collective_id, space, embeddings, cluster, valid):
    docs, width = embeddings.shape
    vmem = pl.BlockSpec(memory_space=pltpu.VMEM)
    dma = pltpu.SemaphoreType.DMA
    slots = [4 * len(group) for group in GROUPS]
    return pl.pallas_call(
        functools.partial(kernel, cap),
        out_shape=(
            jax.ShapeDtypeStruct((1, docs), jnp.float32),
            jax.ShapeDtypeStruct((1, 128), jnp.float32),
            jax.ShapeDtypeStruct((1, docs), jnp.int32),
            jax.ShapeDtypeStruct((1, docs), jnp.int32),
        ),
        in_specs=[pl.BlockSpec(memory_space=space)] * 3,
        out_specs=(vmem,) * 4,
        scratch_shapes=[
            pltpu.VMEM((docs, width), jnp.bfloat16),
            pltpu.VMEM((1, docs), jnp.int32),
            pltpu.VMEM((1, docs), jnp.int32),
            pltpu.VMEM((PLANES, cap // 4, 4, width), jnp.bfloat16),
            pltpu.VMEM((PLANES, 1, 256), jnp.float32),
            pltpu.VMEM((PLANES, cap // 4, 4, width), jnp.bfloat16),
            pltpu.VMEM((PLANES, 1, 256), jnp.float32),
            [pltpu.VMEM((PEERS, n, width), jnp.bfloat16) for n in slots],
            [pltpu.VMEM((PEERS, n, width), jnp.bfloat16) for n in slots],
            [pltpu.VMEM((PEERS * n, 128), jnp.float32) for n in slots],
            [pltpu.VMEM((1, PEERS * n), jnp.float32) for n in slots],
            pltpu.VMEM((2, 8, 128), jnp.float32),
            pltpu.VMEM((PEERS, 8, 128), jnp.float32),
            pltpu.VMEM((8, PEERS * 8), jnp.float32),
            pltpu.VMEM((PLANES, 8, PEERS * 8), jnp.float32),
            dma((PLANES,)),
            dma((PLANES,)),
            dma((PLANES,)),
            dma((PLANES,)),
            dma((len(GROUPS),)),
            dma((len(GROUPS),)),
            dma((len(GROUPS) + 1,)),
            dma(()),
            dma(()),
            dma((PLANES,)),
            dma((PLANES,)),
            dma((3,)),
        ],
        compiler_params=pltpu.CompilerParams(
            collective_id=collective_id, has_side_effects=True, vmem_limit_bytes=40 << 20
        ),
        name=f"route_{cap}",
    )(embeddings, cluster, valid)


def per_device(embeddings, doc_cluster, doc_valid):
    docs = embeddings.shape[0]
    cluster, valid = doc_cluster.reshape(1, docs), doc_valid.reshape(1, docs)
    hbm = [pltpu.with_memory_space_constraint(a, pltpu.HBM) for a in (embeddings, cluster, valid)]
    best, flag, cluster, valid = route(CAP, 0, pltpu.HBM, *hbm)
    best = lax.cond(
        flag[0, 0] > 0.0,
        lambda: route(MOST, 1, pl.ANY, embeddings, cluster, valid)[0],
        lambda: best,
    )
    return best.reshape(docs)


def solution(mesh):
    placed = (P(("shard", "blk"), None), P(("shard", "blk")), P(("shard", "blk")))
    return jax.shard_map(
        per_device, mesh=mesh, in_specs=placed, out_specs=P(("shard", "blk")), check_vma=False
    )
```

```python
import functools
import math

import jax
import jax.numpy as jnp
from jax import lax
from jax.experimental import pallas as pl
from jax.experimental.pallas import tpu as pltpu
from jax.sharding import PartitionSpec as P

MESH = pl.DeviceIdType.MESH
PLANES = 8
PEERS = 32
EMPTY = 2.0
FAR = -8.0

CAP = 52
MOST = 128

STEPS = sorted(
    ((x, y, core) for x in range(4) for y in range(4) for core in range(2) if (x, y, core) != (0, 0, 0)),
    key=lambda step: (-min(step[0], 4 - step[0]) - min(step[1], 4 - step[1]), step),
)
GROUPS = ((0,), (1, 7), (2, 6), (3, 5), (4,))
ORDER = (1, 7, 0, 2, 6, 3, 5, 4)
PLACE = {d: i for i, d in enumerate(d for group in GROUPS for d in group)}


def iota(shape, dim):
    return lax.broadcasted_iota(jnp.int32, shape, dim)


def as_f32(mask):
    return mask.astype(jnp.float32)


def parts(values):
    high = values.astype(jnp.bfloat16)
    rest = values - high.astype(jnp.float32)
    middle = rest.astype(jnp.bfloat16)
    low = (rest - middle.astype(jnp.float32)).astype(jnp.bfloat16)
    return jnp.concatenate([high, middle, low], axis=0)


def kernel(
    cap,
    emb_hbm,
    clus_hbm,
    valid_hbm,
    out_ref,
    flag_ref,
    clus_out,
    valid_out,
    emb_ref,
    clus_ref,
    valid_ref,
    zsend,
    zmeta_send,
    zbuf,
    zmeta,
    psends,
    pbufs,
    biases,
    bests,
    ret_send,
    ret_buf,
    zret_send,
    zret_buf,
    zs_sem,
    zr_sem,
    zms_sem,
    zmr_sem,
    ps_sem,
    pr_sem,
    loc_sem,
    rs_sem,
    rr_sem,
    zrs_sem,
    zrr_sem,
    in_sem,
):
    docs, width = emb_ref.shape
    shard, blk = lax.axis_index("shard"), lax.axis_index("blk")
    my_z = shard // PLANES
    my_p = lax.rem(shard, PLANES) * 4 + blk

    def at(z, p):
        return (z * PLANES + p // 4, lax.rem(p, 4))

    def z_peer(d):
        return at(lax.rem(my_z + d, PLANES), my_p)

    def p_peer(p):
        return at(my_z, p)

    loads = [
        pltpu.make_async_copy(src, dst, in_sem.at[i])
        for i, (src, dst) in enumerate(
            ((emb_hbm, emb_ref), (clus_hbm, clus_ref), (valid_hbm, valid_ref))
        )
    ]
    for load in loads:
        load.start()

    my_x = lax.rem(my_p // 2, 2) * 2 + my_p // 16
    my_y, my_core = lax.rem(my_p // 4, 4), lax.rem(my_p, 2)

    def stepped(step):
        x = lax.rem(my_x + step[0], 4)
        y = lax.rem(my_y + step[1], 4)
        return lax.rem(x, 2) * 16 + y * 4 + (x // 2) * 2 + lax.rem(my_core + step[2], 2)

    barrier = pltpu.get_barrier_semaphore()
    for d in (4, 3, 5, 2, 6, 1, 7):
        pl.semaphore_signal(barrier, inc=1, device_id=z_peer(d), device_id_type=MESH)

    for step in STEPS:
        pl.semaphore_signal(
            barrier, inc=1, device_id=p_peer(stepped(step)), device_id_type=MESH
        )

    for load in loads[1:]:
        load.wait()
    clus = clus_ref[...]
    valid = valid_ref[...] > 0
    clus_out[...] = clus
    valid_out[...] = valid_ref[...]
    owner, sub = clus & 63, clus >> 6
    plane = ((owner >> 3) + 2 * sub) & (PLANES - 1)
    peer_of = (owner & 7) * 4 + sub
    rel = (plane - my_z + PLANES) & (PLANES - 1)
    rel_row = as_f32(jnp.where(valid, rel, -1))
    key_row = as_f32(jnp.where(valid, clus, -1))
    sub_i, lane_i = iota((docs, docs), 0), iota((docs, docs), 1)
    eye = sub_i == lane_i
    earlier = sub_i < lane_i

    def column(row):
        wide = jnp.broadcast_to(row, (docs, docs))
        return jnp.sum(jnp.where(eye, wide, 0.0), axis=1, keepdims=True)

    key_col, rel_col = column(key_row), column(rel_row)
    rank = jnp.sum(as_f32((key_col == key_row) & earlier), axis=0, keepdims=True)
    rank_z = jnp.sum(as_f32((rel_col == rel_row) & earlier), axis=0, keepdims=True)
    slot = {
        n: jnp.broadcast_to(
            jnp.where(valid, as_f32(peer_of * n) + rank + 1.0, 0.0), (8, docs)
        ).astype(jnp.bfloat16)
        for n in (4, 8)
    }
    fits = valid & (rank_z < float(cap))
    overflow = jnp.max(as_f32(valid & (rank_z >= float(cap))), axis=1, keepdims=True)
    target = jnp.where(fits, rel_row * float(cap) + rank_z, -1.0)

    loads[0].wait()
    values = emb_ref[...].astype(jnp.float32)
    scale = lax.rsqrt(jnp.mean(values * values, axis=1, keepdims=True) + 1e-05) / math.sqrt(width)
    unit = (values * scale).astype(jnp.bfloat16)

    pl.semaphore_wait(barrier, PLANES - 1 + PEERS - 1)

    def z_copies(d):
        rows = pltpu.make_async_remote_copy(
            src_ref=zsend.at[d],
            dst_ref=zbuf.at[PLACE[d]],
            send_sem=zs_sem.at[d],
            recv_sem=zr_sem.at[d],
            device_id=z_peer(d),
            device_id_type=MESH,
        )
        meta = pltpu.make_async_remote_copy(
            src_ref=zmeta_send.at[d],
            dst_ref=zmeta.at[d],
            send_sem=zms_sem.at[d],
            recv_sem=zmr_sem.at[d],
            device_id=z_peer(d),
            device_id_type=MESH,
        )
        return rows, meta

    lane128 = iota((1, 128), 1)
    for d in ORDER:
        pick = iota((cap, docs), 0).astype(jnp.float32) + float(d * cap) == target
        pick = as_f32(pick).astype(jnp.bfloat16)
        rows = jnp.dot(pick, unit, preferred_element_type=jnp.float32).astype(jnp.bfloat16)
        meta = lax.dot_general(
            slot[4 if d in (0, 4) else 8], pick, (((1,), (1,)), ((), ())), preferred_element_type=jnp.float32
        )[0:1, :]
        if d == 0:
            zbuf[PLACE[d]] = rows.reshape(cap // 4, 4, width)
            zmeta[d, :, 0:cap] = meta
            zmeta[d, :, 128:256] = jnp.broadcast_to(overflow, (1, 128))
        else:
            zsend[d] = rows.reshape(cap // 4, 4, width)
            zmeta_send[d, :, 0:cap] = meta
            zmeta_send[d, :, 128:256] = jnp.broadcast_to(overflow, (1, 128))
            row_copy, meta_copy = z_copies(d)
            if d != 4:
                meta_copy.start()
                row_copy.start()

    for best in bests:
        best[...] = jnp.full(best.shape, -1.0, jnp.float32)
    flag = jnp.zeros((1, 128), jnp.float32)

    def scatter(g):
        picks = []
        flags = []
        psend, pbuf = psends[g], pbufs[g]
        slots = psend.shape[1]
        slot_lane = iota((PEERS * slots, cap), 0).astype(jnp.float32)
        for h, d in enumerate(GROUPS[g]):
            if d:
                row_copy, meta_copy = z_copies(d)
                meta_copy.wait_recv()
                row_copy.wait_recv()
            meta = zmeta[d, :, 0:cap]
            where_to = jnp.where(meta > 0.0, meta - 1.0 + float(4 * h), -1.0)
            picks.append(as_f32(slot_lane == where_to))
            flags.append(zmeta[d, :, 128:256])
        pick = jnp.concatenate(picks, axis=1) if len(picks) > 1 else picks[0]
        filled = jnp.sum(pick, axis=1, keepdims=True)
        rows = jnp.dot(
            pick.astype(jnp.bfloat16),
            zbuf[PLACE[GROUPS[g][0]] : PLACE[GROUPS[g][-1]] + 1].reshape(len(picks) * cap, width),
            preferred_element_type=jnp.float32,
        )
        mark = jnp.where(iota((PEERS * slots, 128), 1) == 0, EMPTY * (1.0 - filled), 0.0)
        head = (rows[:, 0:128] + mark).astype(jnp.bfloat16)
        psend[:, :, 0:128] = head.reshape(PEERS, slots, 128)
        tail = rows[:, 128:].astype(jnp.bfloat16)
        psend[:, :, 128:] = tail.reshape(PEERS, slots, width - 128)
        local = pltpu.make_async_copy(psend.at[my_p], pbuf.at[my_p], loc_sem.at[g])
        local.start()

        def send(peer):
            pltpu.make_async_remote_copy(
                src_ref=psend.at[peer],
                dst_ref=pbuf.at[my_p],
                send_sem=ps_sem.at[g],
                recv_sem=pr_sem.at[g],
                device_id=p_peer(peer),
                device_id_type=MESH,
            ).start()

        def send_next(i, carry):
            send(lax.rem(my_p + i, PEERS))
            return carry

        if g == len(GROUPS) - 1:
            for step in STEPS:
                send(stepped(step))
        else:
            lax.fori_loop(1, PEERS, send_next, 0)
        return functools.reduce(jnp.maximum, flags)

    def all_in_plane(src, dst, send_sem, recv_sem):
        return pltpu.make_async_remote_copy(
            src_ref=src,
            dst_ref=dst,
            send_sem=send_sem,
            recv_sem=recv_sem,
            device_id=p_peer(lax.rem(my_p + 1, PEERS)),
            device_id_type=MESH,
        )

    def in_plane(g):
        return all_in_plane(
            psends[g].at[pl.ds(0, PEERS - 1)],
            pbufs[g].at[pl.ds(0, PEERS - 1)],
            ps_sem.at[g],
            pr_sem.at[g],
        )

    def rows_of(g):
        return pbufs[g][...].reshape(-1, width)

    def compare(g):
        pltpu.make_async_copy(psends[g].at[my_p], pbufs[g].at[my_p], loc_sem.at[g]).wait()
        in_plane(g).wait_recv()
        mine = rows_of(g)
        first = mine[:, 0:128].astype(jnp.float32)[:, 0:1]
        biases[g][...] = jnp.broadcast_to(jnp.where(first > 1.5, FAR, 0.0), biases[g].shape)

        def block(rows_j, rows_i, j, i):
            similar = lax.dot_general(
                rows_j, rows_i, (((1,), (1,)), ((), ())), preferred_element_type=jnp.float32
            )
            away = biases[j][...]
            if rows_i.shape[0] > 128:
                away = jnp.concatenate([away, away], axis=1)
            similar = similar + away
            if i == j:
                same = iota(similar.shape, 0) == iota(similar.shape, 1)
                similar = jnp.where(same, FAR, similar)
            bests[i][...] = jnp.maximum(bests[i][...], jnp.max(similar, axis=0, keepdims=True))

        block(mine, mine, g, g)
        for j in range(g):
            other = rows_of(j)
            block(other, mine, j, g)
            block(mine, other, g, j)

    for g in range(len(GROUPS)):
        if g == len(GROUPS) - 1:
            compare(0)
        if g == 2:
            for copy in z_copies(4):
                copy.start()
        flag = jnp.maximum(flag, scatter(g))
    for g in range(1, len(GROUPS)):
        compare(g)

    ret_send[...] = jnp.zeros(ret_send.shape, jnp.float32)
    for half in range(2):
        for g, best in enumerate(bests):
            first = half * 128 if best.shape[1] > 128 else 0
            ret_send[half, g : g + 1, :] = best[:, first : first + 128]
        ret_send[half, 5:6, :] = flag
    local = pltpu.make_async_copy(ret_send.at[my_p // 16], ret_buf.at[my_p], loc_sem.at[len(GROUPS)])
    local.start()

    for step in STEPS:
        peer = stepped(step)
        pltpu.make_async_remote_copy(
            src_ref=ret_send.at[peer // 16],
            dst_ref=ret_buf.at[my_p],
            send_sem=rs_sem,
            recv_sem=rr_sem,
            device_id=p_peer(peer),
            device_id_type=MESH,
        ).start()
    number, lane = iota((16, 128), 0), iota((16, 128), 1)
    mine = jnp.where(
        number < 8,
        as_f32(lane == 8 * lax.rem(my_p, 16) + number),
        as_f32((lane == 4 * my_p + number - 8) & (number < 12)),
    ).astype(jnp.bfloat16)
    local.wait()
    all_in_plane(
        ret_buf.at[pl.ds(0, PEERS - 1)], ret_buf.at[pl.ds(0, PEERS - 1)], rs_sem, rr_sem
    ).wait_recv()
    came = ret_buf[...]
    flag_ref[...] = jnp.max(came[:, 5, :], axis=0, keepdims=True)
    back = lax.dot_general(
        mine,
        parts(came.reshape(PEERS * 8, 128)),
        (((1,), (1,)), ((), ())),
        preferred_element_type=jnp.float32,
    )
    back = back[:, 0:256] + back[:, 256:512] + back[:, 512:768]
    group = iota((8, PEERS * 8), 1) & 7
    alone = (group == 0) | (group == len(GROUPS) - 1)
    back = jnp.where(alone, back[8:16], back[0:8])
    zret_buf[0] = back
    zret_send[...] = back

    def z_back(d):
        return pltpu.make_async_remote_copy(
            src_ref=zret_send,
            dst_ref=zret_buf.at[d],
            send_sem=zrs_sem.at[d],
            recv_sem=zrr_sem.at[d],
            device_id=z_peer(PLANES - d),
            device_id_type=MESH,
        )

    for d in (4, 3, 5, 2, 6, 1, 7):
        z_back(d).start()

    upper = rel > 4
    lane_of = as_f32(peer_of * 8 + jnp.where(upper, PLANES - rel, rel))
    row_of = as_f32(rel * 8 + jnp.where(upper, 4, 0)) + rank
    look = as_f32(sub_i.astype(jnp.float32) == lane_of).astype(jnp.bfloat16)
    for d in range(1, PLANES):
        z_back(d).wait_recv()
    found = jnp.dot(
        parts(zret_buf[...].reshape(PLANES * 8, PEERS * 8)),
        look,
        preferred_element_type=jnp.float32,
    )
    found = found[0:64] + found[64:128] + found[128:192]
    right = iota((PLANES * 8, docs), 0).astype(jnp.float32) == row_of
    found = jnp.sum(jnp.where(right, found, 0.0), axis=0, keepdims=True)
    out_ref[...] = jnp.where(valid, jnp.maximum(found, -1.0), -1.0)

    for d in range(1, PLANES):
        row_copy, meta_copy = z_copies(d)
        row_copy.wait_send()
        meta_copy.wait_send()
        z_back(d).wait_send()
    for g in range(len(GROUPS)):
        in_plane(g).wait_send()
    all_in_plane(
        ret_buf.at[pl.ds(0, PEERS - 1)], ret_buf.at[pl.ds(0, PEERS - 1)], rs_sem, rr_sem
    ).wait_send()


def route(cap, collective_id, space, embeddings, cluster, valid):
    docs, width = embeddings.shape
    vmem = pl.BlockSpec(memory_space=pltpu.VMEM)
    dma = pltpu.SemaphoreType.DMA
    slots = [4 * len(group) for group in GROUPS]
    return pl.pallas_call(
        functools.partial(kernel, cap),
        out_shape=(
            jax.ShapeDtypeStruct((1, docs), jnp.float32),
            jax.ShapeDtypeStruct((1, 128), jnp.float32),
            jax.ShapeDtypeStruct((1, docs), jnp.int32),
            jax.ShapeDtypeStruct((1, docs), jnp.int32),
        ),
        in_specs=[pl.BlockSpec(memory_space=space)] * 3,
        out_specs=(vmem,) * 4,
        scratch_shapes=[
            pltpu.VMEM((docs, width), jnp.bfloat16),
            pltpu.VMEM((1, docs), jnp.int32),
            pltpu.VMEM((1, docs), jnp.int32),
            pltpu.VMEM((PLANES, cap // 4, 4, width), jnp.bfloat16),
            pltpu.VMEM((PLANES, 1, 256), jnp.float32),
            pltpu.VMEM((PLANES, cap // 4, 4, width), jnp.bfloat16),
            pltpu.VMEM((PLANES, 1, 256), jnp.float32),
            [pltpu.VMEM((PEERS, n, width), jnp.bfloat16) for n in slots],
            [pltpu.VMEM((PEERS, n, width), jnp.bfloat16) for n in slots],
            [pltpu.VMEM((PEERS * n, 128), jnp.float32) for n in slots],
            [pltpu.VMEM((1, PEERS * n), jnp.float32) for n in slots],
            pltpu.VMEM((2, 8, 128), jnp.float32),
            pltpu.VMEM((PEERS, 8, 128), jnp.float32),
            pltpu.VMEM((8, PEERS * 8), jnp.float32),
            pltpu.VMEM((PLANES, 8, PEERS * 8), jnp.float32),
            dma((PLANES,)),
            dma((PLANES,)),
            dma((PLANES,)),
            dma((PLANES,)),
            dma((len(GROUPS),)),
            dma((len(GROUPS),)),
            dma((len(GROUPS) + 1,)),
            dma(()),
            dma(()),
            dma((PLANES,)),
            dma((PLANES,)),
            dma((3,)),
        ],
        compiler_params=pltpu.CompilerParams(
            collective_id=collective_id, has_side_effects=True, vmem_limit_bytes=40 << 20
        ),
        name=f"route_{cap}",
    )(embeddings, cluster, valid)


def per_device(embeddings, doc_cluster, doc_valid):
    docs = embeddings.shape[0]
    cluster, valid = doc_cluster.reshape(1, docs), doc_valid.reshape(1, docs)
    hbm = [pltpu.with_memory_space_constraint(a, pltpu.HBM) for a in (embeddings, cluster, valid)]
    best, flag, cluster, valid = route(CAP, 0, pltpu.HBM, *hbm)
    best = lax.cond(
        flag[0, 0] > 0.0,
        lambda: route(MOST, 1, pl.ANY, embeddings, cluster, valid)[0],
        lambda: best,
    )
    return best.reshape(docs)


def solution(mesh):
    placed = (P(("shard", "blk"), None), P(("shard", "blk")), P(("shard", "blk")))
    return jax.shard_map(
        per_device, mesh=mesh, in_specs=placed, out_specs=P(("shard", "blk")), check_vma=False
    )
```
